256 devices in a mesh: row: 32 (over z, x), col: 8 (over y, core).
Axes of the slice: x: 4, y: 4, z: 8, core: 2. Of those that a mesh axis runs over, the one named last changes fastest.
Arguments:
- schur: float32 [2, 32768, 4096], P(None, 'row', 'col'), may hold values from -6 to 6
- lower: bfloat16 [2, 32768, 2048], P(None, 'row', 'col'), may hold values from -6 to 6
- upper: bfloat16 [2, 2048, 4096], P(None, 'row', 'col'), may hold values from -0.1875 to 0.1875
- tile_mask: int32 [2, 256, 16], P(None, 'row', 'col'), may hold values from 0 to 1, as said below
- row_map: int32 [2, 32768], P(None, 'row'), may hold values from 0 to 32767, as said below
- front: float32 [32768, 4096], P('row', 'col'), may hold values from -6 to 6
Outputs:
- front_out: float32 [32768, 4096], P('row', 'col')
The draws below stay inside these ranges and needn't reach their ends.
Inputs may be any that keep to these rules, and one draw needn't show every extreme that they name: `tile_mask`: in every row of tiles of each child, each aligned pair of tile columns (2 j, 2 j + 1) holds exactly one 1. `row_map`: for each child a permutation of the 32768 rows. Of the 1024 rows of any aligned block, at least 16 and at most 48 map into any one aligned block of 1024 parent rows; some pair of blocks reaches 48.
All inputs are finite; a program needn't handle non-finite values.
Results may differ from the reference program's by a relative error of at most 0.0003.
Values may be sent and summed in bfloat16 or wider, within the bound.
A program may use at most 128 MiB of HBM per device.

```python
import jax
import jax.numpy as jnp

W = 4096
K = 2048
TILE = 128
CHILDREN = 2
ROWS_DEV = 1024
M = 32768


def draw_tile_mask(key, part):
    picks = jax.random.randint(key, (2, M // TILE, K // (2 * TILE)), 0, 2)
    mask = jnp.stack([1 - picks, picks], axis=-1)
    return mask.reshape(2, M // TILE, K // TILE).astype(jnp.int32)


def single_map(key):
    count = M // ROWS_DEV
    base = ROWS_DEV // count
    spread = base // 2
    keys = jax.random.split(key, 4)
    order = jax.random.permutation(keys[0], count)
    turns = jax.random.randint(keys[1], (count // 2,), 0, spread + 1).astype(jnp.int32)
    turns = turns.at[0].set(spread)
    amounts = jnp.zeros((count,), jnp.int32)
    amounts = amounts.at[order[0::2]].set(base + turns)
    amounts = amounts.at[order[1::2]].set(base - turns)
    offsets = jnp.repeat(jnp.arange(count, dtype=jnp.int32), amounts, total_repeat_length=ROWS_DEV)
    layers = jax.vmap(lambda inner: jax.random.permutation(inner, ROWS_DEV))(jax.random.split(keys[2], count))
    slots = jax.vmap(lambda inner: jax.random.permutation(inner, ROWS_DEV))(jax.random.split(keys[3], count))
    source = jnp.arange(count, dtype=jnp.int32)[:, None]
    target = (source + offsets[layers]) % count
    parent = target * ROWS_DEV + slots[target, layers]
    return parent.reshape(-1).astype(jnp.int32)


def draw_row_map(key, part):
    first = single_map(jax.random.fold_in(key, 11))
    second = single_map(jax.random.fold_in(key, 23))
    return jnp.stack([first, second], axis=0).astype(jnp.int32)


def block_scale(own_key, extent, pieces, smallest, largest):
    loudness, own = 1.0, jax.random.fold_in(own_key, 6)
    for dim, shards_of in pieces:
        draws = jnp.exp(jax.random.uniform(jax.random.fold_in(own, dim), (shards_of,), jnp.float32, smallest / len(pieces), largest / len(pieces)))
        loudness = loudness * jnp.repeat(draws, extent[dim] // shards_of).reshape([-1 if axis == dim else 1 for axis in range(len(extent))])
    return loudness


def normal_values(rng, shape, scale, bound, shards=(), held_as=jnp.bfloat16):
    values = scale * jax.random.normal(rng, shape, jnp.float32)
    if shards:
        values = values * block_scale(rng, shape, shards, -0.22, 0.18)
    return jnp.clip(values, -bound, bound).astype(held_as)


def setup_inputs(seed: int = 0) -> dict:
    seeds = jax.random.split(jax.random.key(seed), 7)
    schur = normal_values(seeds[0], (CHILDREN, M, W), 1.0, 6.0, ((1, 32), (2, 8)), jnp.float32)
    lower = normal_values(seeds[1], (CHILDREN, M, K), 1.0, 6.0, ((1, 32), (2, 8)))
    upper = normal_values(seeds[2], (CHILDREN, K, W), (K // 2) ** -0.5, 0.1875, ((1, 32), (2, 8)))
    tile_mask = draw_tile_mask(jax.random.fold_in(seeds[6], 71), 0)
    row_map = draw_row_map(jax.random.fold_in(seeds[6], 71), 0)
    front = normal_values(seeds[5], (M, W), 1.0, 6.0, ((0, 32), (1, 8)), jnp.float32)
    return dict(schur=schur, lower=lower, upper=upper, tile_mask=tile_mask, row_map=row_map, front=front)


def reference(schur, lower, upper, tile_mask, row_map, front):
    result = front
    for child in range(2):
        mask_full = jnp.repeat(jnp.repeat(tile_mask[child], TILE, axis=0), TILE, axis=1).astype(lower.dtype)
        masked = lower[child] * mask_full
        update = jnp.dot(masked, upper[child], preferred_element_type=jnp.float32)
        contribution = schur[child] - update
        result = result.at[row_map[child]].add(contribution)
    return result
```

```python
import functools

import jax
import jax.numpy as jnp
from jax import lax
from jax.experimental import pallas as pl
from jax.experimental.pallas import tpu as pltpu
from jax.sharding import PartitionSpec as P

TILE = 128
X = 4
CORES = 2
HALVES = 2
MESH = pl.DeviceIdType.MESH
F32 = jnp.float32
BF16 = jnp.bfloat16
I32 = jnp.int32


def dot(a, b):
    return jnp.dot(a, b, preferred_element_type=F32)


def iota(shape, dim):
    return lax.broadcasted_iota(I32, shape, dim)


def kernel(
    dims,
    lower_ref,
    upper_ref,
    mask_ref,
    map_ref,
    schur_hbm,
    front_hbm,
    out_ref,
    schur,
    packed,
    wide,
    panel,
    square,
    hot,
    owner,
    rows_info,
    cols_info,
    place_info,
    scale_col,
    high,
    low,
    code_out,
    code_in,
    meta_out,
    meta_in,
    meta_flat,
    spread,
    high_in,
    low_in,
    local_sem,
    z_send,
    z_recv,
    x_send,
    x_recv,
    y_send,
    y_recv,
    c_send,
    c_recv,
    e_send,
    e_recv,
    m_send,
    m_recv,
):
    count, cols, rows, width, depth, cap = dims
    zs = count // X
    ys = cols // CORES
    cw = width // HALVES
    slots = count * cap
    full = depth * count
    me = lax.axis_index("row")
    col = lax.axis_index("col")
    my_z = me // X
    my_x = lax.rem(me, X)
    my_y = col // CORES
    core = lax.rem(col, CORES)
    partner = my_y * CORES + (1 - core)

    barrier = pltpu.get_barrier_semaphore()

    def greet_row(k, carry):
        pl.semaphore_signal(barrier, inc=1, device_id=(lax.rem(me + k, count), col), device_id_type=MESH)
        return carry

    def greet_col(k, carry):
        pl.semaphore_signal(barrier, inc=1, device_id=(me, lax.rem(col + k, cols)), device_id_type=MESH)
        return carry

    lax.fori_loop(1, count, greet_row, 0)
    lax.fori_loop(1, cols, greet_col, 0)

    schur_copy = pltpu.make_async_copy(schur_hbm, schur, local_sem.at[0])
    front_copy = pltpu.make_async_copy(front_hbm, out_ref, local_sem.at[1])
    schur_copy.start()
    front_copy.start()

    for child in range(2):
        for tile in range(rows // TILE):
            at = pl.ds(tile * TILE, TILE)
            second = mask_ref[child, tile, 1]
            packed[child, col, at, :] = jnp.where(
                second == 1, lower_ref[child, at, TILE : 2 * TILE], lower_ref[child, at, 0:TILE]
            )
        row = iota((16, TILE), 0)
        flags = jnp.zeros((16, TILE), F32)
        for tile in range(rows // TILE):
            flags = jnp.where(row == tile, mask_ref[child, tile, 1].astype(F32), flags)
        packed[child, col, pl.ds(rows, 16), :] = flags.astype(BF16)

    pl.semaphore_wait(barrier, count + cols - 2)

    def upper_block(step):
        child, half = step // HALVES, step % HALVES
        return upper_ref.at[child, :, pl.ds(half * cw, cw)]

    def panel_block(step, z, x):
        start = pl.multiple_of((z * X + x) * depth, depth)
        return panel.at[step, pl.ds(start, depth), :]

    def nearest(n):
        half = n // 2 + 1
        return half + lax.rem(n, 2) * (zs - 2 * half)

    def z_copy(step, dz):
        z = lax.rem(my_z + dz, zs)
        return pltpu.make_async_remote_copy(
            src_ref=upper_block(step),
            dst_ref=panel_block(step, my_z, my_x),
            send_sem=z_send.at[step],
            recv_sem=z_recv.at[step, dz],
            device_id=(z * X + my_x, col),
            device_id_type=MESH,
        )

    def x_copy(step, source, z, dx):
        return pltpu.make_async_remote_copy(
            src_ref=source,
            dst_ref=panel_block(step, z, my_x),
            send_sem=x_send.at[step],
            recv_sem=x_recv.at[step],
            device_id=(my_z * X + lax.rem(my_x + dx, X), col),
            device_id_type=MESH,
        )

    def send_upper(step):
        def body(n, carry):
            z_copy(step, nearest(n)).start()
            return carry

        lax.fori_loop(0, zs - 1, body, 0)
        for dx in (1, 3, 2):
            x_copy(step, upper_block(step), my_z, dx).start()
        pltpu.make_async_copy(upper_block(step), panel_block(step, my_z, my_x), local_sem.at[2 + step]).start()

    def pass_upper(step):
        def body(n, carry):
            dz = nearest(n)
            z_copy(step, dz).wait_recv()
            z = lax.rem(my_z - dz + zs, zs)
            for dx in (1, 3, 2):
                x_copy(step, panel_block(step, z, my_x), z, dx).start()
            return carry

        lax.fori_loop(0, zs - 1, body, 0)

    def wait_upper(step):
        pltpu.make_async_copy(upper_block(step), panel_block(step, my_z, my_x), local_sem.at[2 + step]).wait()
        got = panel.at[step, pl.ds(0, (X - 1) * zs * depth), :]
        pltpu.make_async_remote_copy(
            src_ref=got, dst_ref=got, send_sem=x_send.at[step], recv_sem=x_recv.at[step],
            device_id=(me, partner), device_id_type=MESH,
        ).wait_recv()

    def y_copy(child, dy):
        y = lax.rem(my_y + dy, ys)
        return pltpu.make_async_remote_copy(
            src_ref=packed.at[child, col],
            dst_ref=packed.at[child, col],
            send_sem=y_send.at[child],
            recv_sem=y_recv.at[child, dy],
            device_id=(me, y * CORES + core),
            device_id_type=MESH,
        )

    def c_copy(child, y):
        block = y * CORES + core
        return pltpu.make_async_remote_copy(
            src_ref=packed.at[child, block],
            dst_ref=packed.at[child, block],
            send_sem=c_send.at[child],
            recv_sem=c_recv.at[child],
            device_id=(me, partner),
            device_id_type=MESH,
        )

    def send_lower(child):
        for dy in (1, 3, 2):
            y_copy(child, dy).start()
        c_copy(child, my_y).start()

    def pass_lower(child):
        for dy in (1, 3, 2):
            y_copy(child, dy).wait_recv()
            c_copy(child, lax.rem(my_y - dy + ys, ys)).start()

    def wait_lower(child):
        got = packed.at[child, pl.ds(0, ys)]
        pltpu.make_async_remote_copy(
            src_ref=got, dst_ref=got, send_sem=c_send.at[child], recv_sem=c_recv.at[child],
            device_id=(me, partner), device_id_type=MESH,
        ).wait_recv()

    def index_rows():
        def strict(b, carry):
            at = pl.ds(pl.multiple_of(b * TILE, TILE), TILE)
            before = iota((TILE, rows), 0) + b * TILE < iota((TILE, rows), 1)
            square[at, :] = jnp.where(before, 1.0, 0.0).astype(BF16)
            return carry

        lax.fori_loop(0, rows // TILE, strict, 0)
        for child in range(2):
            line = map_ref[pl.ds(child, 1), :]
            same = iota((count, rows), 0) == line // rows
            owner[child] = jnp.where(same, 1.0, 0.0).astype(BF16)
        rows_info[...] = jnp.zeros_like(rows_info)
        for child in range(2):
            line = map_ref[pl.ds(child, 1), :]
            hits = owner[child]
            ahead = dot(hits, square[...])
            rank = jnp.sum(ahead * hits.astype(F32), axis=0, keepdims=True)
            spot = lax.rem(line, rows) + 1
            rows_info[pl.ds(4 * child, 1), :] = rank
            rows_info[pl.ds(4 * child + 1, 1), :] = (spot // 32).astype(F32)
            rows_info[pl.ds(4 * child + 2, 1), :] = lax.rem(spot, 32).astype(F32)
            rows_info[pl.ds(4 * child + 3, 1), :] = (line // rows).astype(F32)

        def identity(b, carry):
            at = pl.ds(pl.multiple_of(b * TILE, TILE), TILE)
            equal = iota((TILE, rows), 0) + b * TILE == iota((TILE, rows), 1)
            square[at, :] = jnp.where(equal, 1.0, 0.0).astype(BF16)
            return carry

        lax.fori_loop(0, rows // TILE, identity, 0)
        cols_info[...] = lax.dot_general(
            square[...], rows_info[...].astype(BF16), (((1,), (1,)), ((), ())), preferred_element_type=F32
        )
        for child in range(2):
            lane = iota((rows, TILE), 1).astype(F32)
            match = lane - 64.0 == cols_info[:, 4 * child : 4 * child + 1]
            tops = jnp.where(match, cols_info[:, 4 * child + 1 : 4 * child + 2], 0.0).astype(BF16)
            ends = jnp.where(match, cols_info[:, 4 * child + 2 : 4 * child + 3], 0.0).astype(BF16)
            place_info[child] = 32.0 * dot(owner[child], tops) + dot(owner[child], ends)
        slot = iota((TILE, slots), 1).astype(F32)
        inner = slot - cap * jnp.floor((slot + 0.5) * (1.0 / cap))
        lane = iota((TILE, slots), 0).astype(F32)
        spread[0] = jnp.where(lane == inner, 1.0, 0.0).astype(BF16)
        spread[1] = jnp.where(lane - 64.0 == inner, 1.0, 0.0).astype(BF16)

    def build_hot(child):
        flat = rows_info[pl.ds(4 * child + 3, 1), :] * float(cap) + rows_info[pl.ds(4 * child, 1), :]

        def body(b, carry):
            at = pl.ds(pl.multiple_of(b * TILE, TILE), TILE)
            slot = (iota((TILE, rows), 0) + b * TILE).astype(F32)
            hot[at, :] = jnp.where(slot == flat, 1.0, 0.0).astype(BF16)
            return carry

        lax.fori_loop(0, slots // TILE, body, 0)

    def widen(child):
        def body(j, carry):
            flags = packed[child, j, pl.ds(rows, 16), :].astype(F32)
            for tile in range(rows // TILE):
                at = pl.ds(tile * TILE, TILE)
                block = packed[child, j, at, :].astype(F32)
                flag = flags[tile : tile + 1, :]
                left = pl.multiple_of(j * 2 * TILE, TILE)
                right = pl.multiple_of(j * 2 * TILE + TILE, TILE)
                wide[at, pl.ds(left, TILE)] = (block * (1.0 - flag)).astype(BF16)
                wide[at, pl.ds(right, TILE)] = (block * flag).astype(BF16)
            return carry

        lax.fori_loop(0, cols, body, 0)

    def contribute(step):
        child, half = step // HALVES, step % HALVES
        part = rows // 2
        for b in range(2):
            at = pl.ds(b * part, part)
            update = dot(wide[at, :], panel[step])
            value = schur[child, at, pl.ds(half * cw, cw)] - update
            peak = jnp.maximum(jnp.max(jnp.abs(value), axis=1, keepdims=True), 1e-30)
            scale_col[at, :] = jnp.broadcast_to(peak * ((1.0 + 2.0**-8) / 32767.0), (part, TILE)).astype(BF16)
            inverse = 1.0 / scale_col[at, :].astype(F32)
            code = jnp.floor(value * inverse[:, 0:1] + 0.5)
            top = jnp.floor(code * (1.0 / 256.0))
            high[at, :] = top.astype(BF16)
            low[at, :] = (code - 256.0 * top).astype(BF16)
        size = slots // 3
        for b in range(3):
            at = pl.ds(b * size, size)
            code = 256.0 * dot(hot[at, :], high[...]) + dot(hot[at, :], low[...])
            code_out[step, at, :] = code.astype(I32).astype(jnp.int16)
        lane = iota((rows, TILE), 1).astype(F32)
        match = lane == cols_info[:, 4 * child : 4 * child + 1]
        scales = jnp.where(match, scale_col[...].astype(F32), 0.0).astype(BF16)
        meta = dot(owner[child], scales) + place_info[child]
        for t in range(count):
            meta_out[step, t] = meta[t : t + 1, :]

    def rows_of(t):
        return pl.ds(pl.multiple_of(t * cap, 16), cap)

    def e_copy(step, k):
        t = lax.rem(me + k, count)
        return pltpu.make_async_remote_copy(
            src_ref=code_out.at[step, rows_of(t), :],
            dst_ref=code_in.at[step, rows_of(me), :],
            send_sem=e_send.at[step],
            recv_sem=e_recv.at[step],
            device_id=(t, col),
            device_id_type=MESH,
        )

    def m_copy(step, k):
        t = lax.rem(me + k, count)
        return pltpu.make_async_remote_copy(
            src_ref=meta_out.at[step, t],
            dst_ref=meta_in.at[step, me],
            send_sem=m_send.at[step],
            recv_sem=m_recv.at[step],
            device_id=(t, col),
            device_id_type=MESH,
        )

    def own_copies(step):
        return (
            pltpu.make_async_copy(
                code_out.at[step, rows_of(me), :], code_in.at[step, rows_of(me), :], local_sem.at[6 + step]
            ),
            pltpu.make_async_copy(meta_out.at[step, me], meta_in.at[step, me], local_sem.at[10 + step]),
        )

    def exchange(step):
        def body(k, carry):
            e_copy(step, k).start()
            m_copy(step, k).start()
            return carry

        lax.fori_loop(1, count, body, 0)
        for copy in own_copies(step):
            copy.start()

    def all_codes(step):
        got = code_in.at[step, pl.ds(0, (count - 1) * cap), :]
        return pltpu.make_async_remote_copy(
            src_ref=got, dst_ref=got, send_sem=e_send.at[step], recv_sem=e_recv.at[step],
            device_id=(me, partner), device_id_type=MESH,
        )

    def all_meta(step):
        got = meta_in.at[step, pl.ds(0, count - 1)]
        return pltpu.make_async_remote_copy(
            src_ref=got, dst_ref=got, send_sem=m_send.at[step], recv_sem=m_recv.at[step],
            device_id=(me, partner), device_id_type=MESH,
        )

    def collect(step):
        half = step % HALVES
        for copy in own_copies(step):
            copy.wait()
        all_codes(step).wait_recv()
        all_meta(step).wait_recv()
        for s in range(count):
            meta_flat[s : s + 1, :] = meta_in[step, s]
        flat = meta_flat[...]
        tops = jnp.floor(flat * (1.0 / 32.0))
        ends = flat - 32.0 * tops
        places = 32.0 * dot(tops.astype(BF16), spread[1]) + dot(ends.astype(BF16), spread[1])
        scales = dot(flat.astype(BF16), spread[0])
        slot = iota((count, slots), 1)
        first = iota((count, slots), 0) * cap
        own = (slot >= first) & (slot < first + cap)
        place = jnp.sum(jnp.where(own, places, 0.0), axis=0, keepdims=True)
        scale = jnp.sum(jnp.where(own, scales, 0.0), axis=0, keepdims=True)
        size = slots // 3
        for b in range(3):
            at = pl.ds(b * size, size)
            code = code_in[step, at, :].astype(I32)
            high_in[at, :] = (code >> 8).astype(F32).astype(BF16)
            low_in[at, :] = (code & 255).astype(F32).astype(BF16)
        part = rows // 4
        for b in range(4):
            target = (iota((part, slots), 0) + (b * part + 1)).astype(F32)
            pick = jnp.where(target == place, scale, 0.0).astype(BF16)
            at = (pl.ds(b * part, part), pl.ds(half * cw, cw))
            out_ref[at] = out_ref[at] + (256.0 * dot(pick, high_in[...]) + dot(pick, low_in[...]))

    send_upper(0)
    send_lower(0)
    send_upper(1)
    index_rows()
    pass_upper(0)
    pass_lower(0)
    send_lower(1)
    send_upper(2)
    send_upper(3)
    build_hot(0)
    pass_upper(1)
    wait_lower(0)
    widen(0)
    schur_copy.wait()
    wait_upper(0)
    contribute(0)
    exchange(0)
    pass_upper(2)
    pass_lower(1)
    wait_upper(1)
    contribute(1)
    exchange(1)
    pass_upper(3)
    wait_lower(1)
    widen(1)
    build_hot(1)
    wait_upper(2)
    contribute(2)
    exchange(2)
    front_copy.wait()
    collect(0)
    wait_upper(3)
    contribute(3)
    exchange(3)
    collect(1)
    collect(2)
    collect(3)

    for step in range(2 * HALVES):
        sent = panel.at[step, pl.ds(0, (zs - 1) * depth), :]
        pltpu.make_async_remote_copy(
            src_ref=sent, dst_ref=sent, send_sem=z_send.at[step], recv_sem=z_recv.at[step, 0],
            device_id=(me, partner), device_id_type=MESH,
        ).wait_send()
        sent = panel.at[step, pl.ds(0, (X - 1) * zs * depth), :]
        pltpu.make_async_remote_copy(
            src_ref=sent, dst_ref=sent, send_sem=x_send.at[step], recv_sem=x_recv.at[step],
            device_id=(me, partner), device_id_type=MESH,
        ).wait_send()
        all_codes(step).wait_send()
        all_meta(step).wait_send()
    for child in range(2):
        sent = packed.at[child, pl.ds(0, ys - 1)]
        pltpu.make_async_remote_copy(
            src_ref=sent, dst_ref=sent, send_sem=y_send.at[child], recv_sem=y_recv.at[child, 0],
            device_id=(me, partner), device_id_type=MESH,
        ).wait_send()
        sent = packed.at[child, pl.ds(0, ys)]
        pltpu.make_async_remote_copy(
            src_ref=sent, dst_ref=sent, send_sem=c_send.at[child], recv_sem=c_recv.at[child],
            device_id=(me, partner), device_id_type=MESH,
        ).wait_send()


def shards(count, cols, schur, lower, upper, tile_mask, row_map, front):
    children, rows, _ = lower.shape
    width = schur.shape[2]
    depth = upper.shape[1]
    cap = 3 * rows // (2 * count)
    slots = count * cap
    cw = width // HALVES
    steps = children * HALVES
    full = depth * count
    zs = count // X
    ys = cols // CORES
    dims = (count, cols, rows, width, depth, cap)
    vmem = pl.BlockSpec(memory_space=pltpu.VMEM)
    hbm = pl.BlockSpec(memory_space=pl.ANY)
    dma = pltpu.SemaphoreType.DMA
    return pl.pallas_call(
        functools.partial(kernel, dims),
        out_shape=jax.ShapeDtypeStruct((rows, width), F32),
        in_specs=[vmem, vmem, pl.BlockSpec(memory_space=pltpu.SMEM), vmem, hbm, hbm],
        out_specs=vmem,
        scratch_shapes=[
            pltpu.VMEM((children, rows, width), F32),
            pltpu.VMEM((children, cols, rows + 16, TILE), BF16),
            pltpu.VMEM((rows, full), BF16),
            pltpu.VMEM((steps, full, cw), BF16),
            pltpu.VMEM((rows, rows), BF16),
            pltpu.VMEM((slots, rows), BF16),
            pltpu.VMEM((children, count, rows), BF16),
            pltpu.VMEM((8, rows), F32),
            pltpu.VMEM((rows, 8), F32),
            pltpu.VMEM((children, count, TILE), F32),
            pltpu.VMEM((rows, TILE), BF16),
            pltpu.VMEM((rows, cw), BF16),
            pltpu.VMEM((rows, cw), BF16),
            pltpu.VMEM((steps, slots, cw), jnp.int16),
            pltpu.VMEM((steps, slots, cw), jnp.int16),
            pltpu.VMEM((steps, count, 1, TILE), F32),
            pltpu.VMEM((steps, count, 1, TILE), F32),
            pltpu.VMEM((count, TILE), F32),
            pltpu.VMEM((2, TILE, slots), BF16),
            pltpu.VMEM((slots, cw), BF16),
            pltpu.VMEM((slots, cw), BF16),
            dma((14,)),
            dma((steps,)),
            dma((steps, zs)),
            dma((steps,)),
            dma((steps,)),
            dma((children,)),
            dma((children, ys)),
            dma((children,)),
            dma((children,)),
            dma((steps,)),
            dma((steps,)),
            dma((steps,)),
            dma((steps,)),
        ],
        compiler_params=pltpu.CompilerParams(
            collective_id=0, has_side_effects=True, vmem_limit_bytes=60 * 2**20
        ),
    )(lower, upper, tile_mask, row_map, schur, front)


def solution(mesh):
    count, cols = mesh.shape["row"], mesh.shape["col"]
    split = P(None, "row", "col")
    return jax.shard_map(
        functools.partial(shards, count, cols),
        mesh=mesh,
        in_specs=(split, split, split, split, P(None, "row"), P("row", "col")),
        out_specs=P("row", "col"),
        check_vma=False,
    )
```

```python
import functools

import jax
import jax.numpy as jnp
from jax import lax
from jax.experimental import pallas as pl
from jax.experimental.pallas import tpu as pltpu
from jax.sharding import PartitionSpec as P

TILE = 128
X = 4
CORES = 2
STEPS = ((0, 0, 1), (0, 1, 1), (0, 2, 2), (1, 0, 2), (1, 2, 2))
DIRECT = 2
GROUPS = 2
MESH = pl.DeviceIdType.MESH
F32 = jnp.float32
BF16 = jnp.bfloat16
I32 = jnp.int32


def dot(a, b):
    return jnp.dot(a, b, preferred_element_type=F32)


def iota(shape, dim):
    return lax.broadcasted_iota(I32, shape, dim)


def kernel(
    dims,
    lower_hbm,
    upper_hbm,
    mask_ref,
    map_ref,
    schur_hbm,
    out_ref,
    s,
):
    count, cols, rows, width, depth, cap = dims
    zs = count // X
    ys = cols // CORES
    quarter = width // 4
    slots = count * cap
    steps = len(STEPS)
    members = count // GROUPS
    me = lax.axis_index("row")
    col = lax.axis_index("col")
    my_z = me // X
    my_x = lax.rem(me, X)
    my_y = col // CORES
    core = lax.rem(col, CORES)
    partner = my_y * CORES + (1 - core)
    lower, upper, schur, packed, wide, panel = s["lower"], s["upper"], s["schur"], s["packed"], s["wide"], s["panel"]
    square, hot, owner = s["square"], s["hot"], s["owner"]
    rows_info, cols_info, place_info = s["rows_info"], s["cols_info"], s["place_info"]
    scale_col, high, low = s["scale_col"], s["high"], s["low"]
    code_out, code_in, meta_out, meta_in = s["code_out"], s["code_in"], s["meta_out"], s["meta_in"]
    meta_flat, spread, high_in, low_in = s["meta_flat"], s["spread"], s["high_in"], s["low_in"]
    local_sem = s["local_sem"]

    barrier = pltpu.get_barrier_semaphore()

    def greet_row(k, carry):
        pl.semaphore_signal(barrier, inc=1, device_id=(lax.rem(me + k, count), col), device_id_type=MESH)
        return carry

    def greet_col(k, carry):
        pl.semaphore_signal(barrier, inc=1, device_id=(me, lax.rem(col + k, cols)), device_id_type=MESH)
        return carry

    lax.fori_loop(1, count, greet_row, 0)
    lax.fori_loop(1, cols, greet_col, 0)

    lower_copy = pltpu.make_async_copy(lower_hbm, lower, local_sem.at[1])
    upper_copy = pltpu.make_async_copy(upper_hbm, upper, local_sem.at[2])
    schur_copy = pltpu.make_async_copy(schur_hbm, schur, local_sem.at[0])
    lower_copy.start()
    upper_copy.start()
    schur_copy.start()

    def remote(source, target, sent, got, device):
        return pltpu.make_async_remote_copy(
            src_ref=source, dst_ref=target, send_sem=sent, recv_sem=got, device_id=device, device_id_type=MESH
        )

    def total(ref, sent, got):
        return remote(ref, ref, sent, got, (me, partner))

    def pack(child):
        for tile in range(rows // TILE):
            at = pl.ds(tile * TILE, TILE)
            second = mask_ref[child, 1, tile]
            packed[child, col, at, :] = jnp.where(
                second == 1, lower[child, at, TILE : 2 * TILE], lower[child, at, 0:TILE]
            )
        row = iota((16, TILE), 0)
        flags = jnp.zeros((16, TILE), F32)
        for tile in range(rows // TILE):
            flags = jnp.where(row == tile, mask_ref[child, 1, tile].astype(F32), flags)
        packed[child, col, pl.ds(rows, 16), :] = flags.astype(BF16)

    def upper_block(step):
        child, first, number = STEPS[step]
        return upper.at[child, :, pl.ds(first * quarter, number * quarter)]

    def panel_block(step, z, x):
        start = pl.multiple_of((z * X + x) * depth, depth)
        return panel[step].at[pl.ds(start, depth), :]

    def nearest(n):
        half = n // 2 + 1
        return half + lax.rem(n, 2) * (zs - 2 * half)

    def z_copy(step, dz):
        z = lax.rem(my_z + dz, zs)
        return remote(
            upper_block(step),
            panel_block(step, my_z, my_x),
            s["z_send"].at[step],
            s["z_recv"].at[step, dz],
            (z * X + my_x, col),
        )

    def x_copy(step, source, z, dx):
        return remote(
            source,
            panel_block(step, z, my_x),
            s["x_send"].at[step],
            s["x_recv"].at[step],
            (my_z * X + lax.rem(my_x + dx, X), col),
        )

    def send_own(step):
        for dx in (1, 3, 2):
            x_copy(step, upper_block(step), my_z, dx).start()
        pltpu.make_async_copy(upper_block(step), panel_block(step, my_z, my_x), local_sem.at[3 + step]).start()

    def send_upper(step):
        def body(n, carry):
            z_copy(step, nearest(n)).start()
            return carry

        lax.fori_loop(0, zs - 1, body, 0)
        send_own(step)

    def pass_upper(step):
        def body(n, carry):
            dz = nearest(n)
            z_copy(step, dz).wait_recv()
            z = lax.rem(my_z - dz + zs, zs)
            for dx in (1, 3, 2):
                x_copy(step, panel_block(step, z, my_x), z, dx).start()
            return carry

        lax.fori_loop(0, zs - 1, body, 0)

    def reach(step, way):
        return zs // 2 if (step % 2 == 0) == (way > 0) else zs // 2 - 1

    def hop_copy(step, way, hop):
        z = lax.rem(my_z - way * (hop - 1) + zs, zs)
        block = upper_block(step) if hop == 1 else panel_block(step, z, my_x)
        return remote(
            block,
            panel_block(step, z, my_x),
            s["z_send"].at[step],
            s["z_recv"].at[step, (way * hop) % zs],
            (lax.rem(my_z + way + zs, zs) * X + my_x, col),
        )

    def hop_wait(step, hop):
        for way in (1, -1):
            if hop <= reach(step, way):
                hop_copy(step, way, hop).wait_recv()

    def hop_send(step, hop):
        for way in (1, -1):
            if hop <= reach(step, way):
                hop_copy(step, way, hop).start()

    def hops(hop):
        for step in range(DIRECT, steps):
            hop_wait(step, hop)
            hop_send(step, hop + 1)

    def x_spread(step):
        send_own(step)

        def body(n, carry):
            z = lax.rem(my_z + n, zs)
            for dx in (1, 3, 2):
                x_copy(step, panel_block(step, z, my_x), z, dx).start()
            return carry

        lax.fori_loop(1, zs, body, 0)

    def all_x(step):
        return total(
            panel[step].at[pl.ds(0, (X - 1) * zs * depth), :], s["x_send"].at[step], s["x_recv"].at[step]
        )

    def wait_upper(step):
        pltpu.make_async_copy(upper_block(step), panel_block(step, my_z, my_x), local_sem.at[3 + step]).wait()
        all_x(step).wait_recv()

    middle = rows // 2
    parts = (pl.ds(0, middle), pl.ds(middle, rows + 16 - middle))

    def y_copy(child, way, part, hop):
        block = lax.rem(my_y - way * (hop - 1) + ys, ys) * CORES + core
        ref = packed.at[child, block, parts[part], :]
        return remote(
            ref,
            ref,
            s["y_send"].at[child, (1 + way) // 2, part, hop - 1],
            s["y_recv"].at[child, (1 + way) // 2, part, hop - 1],
            (me, lax.rem(my_y + way + ys, ys) * CORES + core),
        )

    def c_copy(child, behind, part):
        block = lax.rem(my_y - behind + ys, ys) * CORES + core
        ref = packed.at[child, block, parts[part], :]
        return remote(ref, ref, s["c_send"].at[child], s["c_recv"].at[child], (me, partner))

    def send_lower(child):
        for way, part in ((1, 0), (-1, 1), (1, 1), (-1, 0)):
            y_copy(child, way, part, 1).start()
        for part in range(2):
            c_copy(child, 0, part).start()

    def pass_lower(child):
        for way, part in ((1, 0), (-1, 1)):
            y_copy(child, way, part, 1).wait_recv()
            y_copy(child, way, part, 2).start()
            c_copy(child, way, part).start()

    def pass_lower_again(child):
        for way, part in ((1, 1), (-1, 0)):
            y_copy(child, way, part, 1).wait_recv()
            c_copy(child, way, part).start()
        for way, part in ((1, 0), (-1, 1)):
            y_copy(child, way, part, 2).wait_recv()
            c_copy(child, 2 * way, part).start()

    def all_c(child):
        return total(packed.at[child, pl.ds(0, ys)], s["c_send"].at[child], s["c_recv"].at[child])

    def index_rows():
        def strict(b, carry):
            at = pl.ds(pl.multiple_of(b * TILE, TILE), TILE)
            before = iota((TILE, rows), 0) + b * TILE < iota((TILE, rows), 1)
            square[at, :] = jnp.where(before, 1.0, 0.0).astype(BF16)
            return carry

        lax.fori_loop(0, rows // TILE, strict, 0)
        for child in range(2):
            line = map_ref[pl.ds(child, 1), :]
            same = iota((count, rows), 0) == line // rows
            owner[child] = jnp.where(same, 1.0, 0.0).astype(BF16)
        rows_info[...] = jnp.zeros_like(rows_info)
        for child in range(2):
            line = map_ref[pl.ds(child, 1), :]
            hits = owner[child]
            ahead = dot(hits, square[...])
            rank = jnp.sum(ahead * hits.astype(F32), axis=0, keepdims=True)
            spot = lax.rem(line, rows) + 1
            rows_info[pl.ds(4 * child, 1), :] = rank
            rows_info[pl.ds(4 * child + 1, 1), :] = (spot // 32).astype(F32)
            rows_info[pl.ds(4 * child + 2, 1), :] = lax.rem(spot, 32).astype(F32)
            rows_info[pl.ds(4 * child + 3, 1), :] = (line // rows).astype(F32)

        def identity(b, carry):
            at = pl.ds(pl.multiple_of(b * TILE, TILE), TILE)
            equal = iota((TILE, rows), 0) + b * TILE == iota((TILE, rows), 1)
            square[at, :] = jnp.where(equal, 1.0, 0.0).astype(BF16)
            return carry

        lax.fori_loop(0, rows // TILE, identity, 0)
        cols_info[...] = lax.dot_general(
            square[...], rows_info[...].astype(BF16), (((1,), (1,)), ((), ())), preferred_element_type=F32
        )
        for child in range(2):
            lane = iota((rows, TILE), 1).astype(F32)
            match = lane - 64.0 == cols_info[:, 4 * child : 4 * child + 1]
            tops = jnp.where(match, cols_info[:, 4 * child + 1 : 4 * child + 2], 0.0).astype(BF16)
            ends = jnp.where(match, cols_info[:, 4 * child + 2 : 4 * child + 3], 0.0).astype(BF16)
            place_info[child] = 32.0 * dot(owner[child], tops) + dot(owner[child], ends)
        slot = iota((TILE, members * cap), 1).astype(F32)
        inner = slot - cap * jnp.floor((slot + 0.5) * (1.0 / cap))
        lane = iota((TILE, members * cap), 0).astype(F32)
        spread[0] = jnp.where(lane == inner, 1.0, 0.0).astype(BF16)
        spread[1] = jnp.where(lane - 64.0 == inner, 1.0, 0.0).astype(BF16)

    def build_hot(child):
        flat = rows_info[pl.ds(4 * child + 3, 1), :] * float(cap) + rows_info[pl.ds(4 * child, 1), :]

        def body(b, carry):
            at = pl.ds(pl.multiple_of(b * TILE, TILE), TILE)
            slot = (iota((TILE, rows), 0) + b * TILE).astype(F32)
            hot[at, :] = jnp.where(slot == flat, 1.0, 0.0).astype(BF16)
            return carry

        lax.fori_loop(0, slots // TILE, body, 0)

    def widen(child):
        def body(j, carry):
            flags = packed[child, j, pl.ds(rows, 16), :].astype(F32)
            for tile in range(rows // TILE):
                at = pl.ds(tile * TILE, TILE)
                block = packed[child, j, at, :].astype(F32)
                flag = flags[tile : tile + 1, :]
                left = pl.multiple_of(j * 2 * TILE, TILE)
                right = pl.multiple_of(j * 2 * TILE + TILE, TILE)
                wide[at, pl.ds(left, TILE)] = (block * (1.0 - flag)).astype(BF16)
                wide[at, pl.ds(right, TILE)] = (block * flag).astype(BF16)
            return carry

        lax.fori_loop(0, cols, body, 0)

    def contribute(step):
        child, first, number = STEPS[step]
        cw = number * quarter
        part = rows // 2
        for b in range(2):
            at = pl.ds(b * part, part)
            update = dot(wide[at, :], panel[step][...])
            value = schur[child, at, pl.ds(first * quarter, cw)] - update
            peak = jnp.maximum(jnp.max(jnp.abs(value), axis=1, keepdims=True), 1e-30)
            scale_col[at, :] = jnp.broadcast_to(peak * ((1.0 + 2.0**-8) / 32767.0), (part, TILE)).astype(BF16)
            inverse = 1.0 / scale_col[at, :].astype(F32)
            code = jnp.floor(value * inverse[:, 0:1] + 0.5)
            top = jnp.floor(code * (1.0 / 256.0))
            high[at, 0:cw] = top.astype(BF16)
            low[at, 0:cw] = (code - 256.0 * top).astype(BF16)
        size = slots // 3
        for b in range(3):
            at = pl.ds(b * size, size)
            code = 256.0 * dot(hot[at, :], high[:, 0:cw]) + dot(hot[at, :], low[:, 0:cw])
            code_out[step][at, :] = code.astype(I32).astype(jnp.int16)
        lane = iota((rows, TILE), 1).astype(F32)
        match = lane == cols_info[:, 4 * child : 4 * child + 1]
        scales = jnp.where(match, scale_col[...].astype(F32), 0.0).astype(BF16)
        meta = dot(owner[child], scales) + place_info[child]
        for t in range(count):
            meta_out[step, t] = meta[t : t + 1, :]

    def rows_of(t):
        return pl.ds(pl.multiple_of(t * cap, 16), cap)

    def shift(n):
        place = n // 2 + lax.rem(n, 2) * (count - 2 - 2 * (n // 2))
        half = place // 2 + 1
        return half + lax.rem(place, 2) * (count - 2 * half)

    def e_copy(step, n, group):
        t = lax.rem(me + shift(n), count)
        return remote(
            code_out[step].at[rows_of(t), :],
            code_in[step].at[rows_of(n), :],
            s["e_send"].at[step],
            s["e_recv"].at[step, group],
            (t, col),
        )

    def m_copy(step, n, group):
        t = lax.rem(me + shift(n), count)
        return remote(
            meta_out.at[step, t], meta_in.at[step, n], s["m_send"].at[step], s["m_recv"].at[step, group], (t, col)
        )

    def own_copies(step):
        return (
            pltpu.make_async_copy(
                code_out[step].at[rows_of(me), :], code_in[step].at[rows_of(count - 1), :], local_sem.at[8 + step]
            ),
            pltpu.make_async_copy(meta_out.at[step, me], meta_in.at[step, count - 1], local_sem.at[13 + step]),
        )

    def exchange(step):
        for group in range(GROUPS):

            def body(n, carry):
                m_copy(step, n, group).start()
                e_copy(step, n, group).start()
                return carry

            lax.fori_loop(group * members, min((group + 1) * members, count - 1), body, 0)
        for copy in own_copies(step):
            copy.start()

    def all_codes(step, group, number):
        ref = code_in[step].at[pl.ds(0, number * cap), :]
        return total(ref, s["e_send"].at[step], s["e_recv"].at[step, group])

    def all_meta(step, group, number):
        ref = meta_in.at[step, pl.ds(0, number)]
        return total(ref, s["m_send"].at[step], s["m_recv"].at[step, group])

    def collect(step, group):
        _, first, number = STEPS[step]
        cw = number * quarter
        others = members
        if group == GROUPS - 1:
            others = members - 1
            for copy in own_copies(step):
                copy.wait()
        all_meta(step, group, others).wait_recv()
        for m in range(members):
            meta_flat[m : m + 1, :] = meta_in[step, group * members + m]
        flat = meta_flat[...]
        tops = jnp.floor(flat * (1.0 / 32.0))
        ends = flat - 32.0 * tops
        places = 32.0 * dot(tops.astype(BF16), spread[1]) + dot(ends.astype(BF16), spread[1])
        scales = dot(flat.astype(BF16), spread[0])
        size = members * cap
        slot = iota((members, size), 1)
        start = iota((members, size), 0) * cap
        own = (slot >= start) & (slot < start + cap)
        place = jnp.sum(jnp.where(own, places, 0.0), axis=0, keepdims=True)
        scale = jnp.sum(jnp.where(own, scales, 0.0), axis=0, keepdims=True)
        all_codes(step, group, others).wait_recv()
        code = code_in[step][group * size : (group + 1) * size, :].astype(I32)
        high_in[:, 0:cw] = (code >> 8).astype(F32).astype(BF16)
        low_in[:, 0:cw] = (code & 255).astype(F32).astype(BF16)
        part = rows // 2
        for b in range(2):
            target = (iota((part, size), 0) + (b * part + 1)).astype(F32)
            pick = jnp.where(target == place, scale, 0.0).astype(BF16)
            at = (pl.ds(b * part, part), pl.ds(first * quarter, cw))
            value = 256.0 * dot(pick, high_in[:, 0:cw]) + dot(pick, low_in[:, 0:cw])
            if STEPS[step][0] == 0 and group == 0:
                out_ref[at] = value
            else:
                out_ref[at] = out_ref[at] + value

    lower_copy.wait()
    upper_copy.wait()
    pack(0)
    pl.semaphore_wait(barrier, count + cols - 2)
    send_upper(0)
    send_lower(0)
    send_upper(1)
    for step in range(DIRECT, steps):
        hop_send(step, 1)
    pack(1)
    index_rows()
    pass_upper(0)
    pass_lower(0)
    pass_upper(1)
    hops(1)
    pass_lower_again(0)
    send_lower(1)
    build_hot(0)
    hops(2)
    all_c(0).wait_recv()
    widen(0)
    schur_copy.wait()
    hops(3)
    wait_upper(0)
    contribute(0)
    exchange(0)
    for step in range(DIRECT, steps):
        hop_wait(step, 4)
    x_spread(2)
    pass_lower(1)
    wait_upper(1)
    contribute(1)
    exchange(1)
    x_spread(3)
    pass_lower_again(1)
    wait_upper(2)
    contribute(2)
    exchange(2)
    x_spread(4)
    all_c(1).wait_recv()
    widen(1)
    build_hot(1)
    collect(0, 0)
    collect(0, 1)
    wait_upper(3)
    contribute(3)
    exchange(3)
    collect(1, 0)
    collect(1, 1)
    wait_upper(4)
    contribute(4)
    exchange(4)
    for step in range(2, steps):
        for group in range(GROUPS):
            collect(step, group)

    for step in range(steps):
        total(
            panel[step].at[pl.ds(0, (zs - 1) * depth), :], s["z_send"].at[step], s["z_recv"].at[step, 0]
        ).wait_send()
        all_x(step).wait_send()
        all_codes(step, 0, count - 1).wait_send()
        all_meta(step, 0, count - 1).wait_send()
    for child in range(2):
        for part in range(2):
            for way in (1, -1):
                y_copy(child, way, part, 1).wait_send()
            y_copy(child, 1 - 2 * part, part, 2).wait_send()
        all_c(child).wait_send()


def shards(count, cols, schur, lower, upper, tile_mask, row_map, front):
    children, rows, _ = lower.shape
    width = schur.shape[2]
    depth = upper.shape[1]
    cap = 3 * rows // (2 * count)
    slots = count * cap
    steps = len(STEPS)
    full = depth * count
    zs = count // X
    members = count // GROUPS
    dims = (count, cols, rows, width, depth, cap)
    widths = [width // 4 * number for _, _, number in STEPS]
    half = width // 2
    vmem = pl.BlockSpec(memory_space=pltpu.VMEM)
    hbm = pl.BlockSpec(memory_space=pltpu.HBM)
    dma = pltpu.SemaphoreType.DMA
    scratch = dict(
        lower=pltpu.VMEM(lower.shape, BF16),
        upper=pltpu.VMEM(upper.shape, BF16),
        schur=pltpu.VMEM(schur.shape, F32),
        packed=pltpu.VMEM((children, cols, rows + 16, TILE), BF16),
        wide=pltpu.VMEM((rows, full), BF16),
        panel=[pltpu.VMEM((full, w), BF16) for w in widths],
        square=pltpu.VMEM((rows, rows), BF16),
        hot=pltpu.VMEM((slots, rows), BF16),
        owner=pltpu.VMEM((children, count, rows), BF16),
        rows_info=pltpu.VMEM((8, rows), F32),
        cols_info=pltpu.VMEM((rows, 8), F32),
        place_info=pltpu.VMEM((children, count, TILE), F32),
        scale_col=pltpu.VMEM((rows, TILE), BF16),
        high=pltpu.VMEM((rows, half), BF16),
        low=pltpu.VMEM((rows, half), BF16),
        code_out=[pltpu.VMEM((slots, w), jnp.int16) for w in widths],
        code_in=[pltpu.VMEM((slots, w), jnp.int16) for w in widths],
        meta_out=pltpu.VMEM((steps, count, 1, TILE), F32),
        meta_in=pltpu.VMEM((steps, count, 1, TILE), F32),
        meta_flat=pltpu.VMEM((members, TILE), F32),
        spread=pltpu.VMEM((2, TILE, members * cap), BF16),
        high_in=pltpu.VMEM((members * cap, half), BF16),
        low_in=pltpu.VMEM((members * cap, half), BF16),
        local_sem=dma((18,)),
        z_send=dma((steps,)),
        z_recv=dma((steps, zs)),
        x_send=dma((steps,)),
        x_recv=dma((steps,)),
        y_send=dma((children, 2, 2, 2)),
        y_recv=dma((children, 2, 2, 2)),
        c_send=dma((children,)),
        c_recv=dma((children,)),
        e_send=dma((steps,)),
        e_recv=dma((steps, GROUPS)),
        m_send=dma((steps,)),
        m_recv=dma((steps, GROUPS)),
    )
    added = pl.pallas_call(
        functools.partial(kernel, dims),
        out_shape=jax.ShapeDtypeStruct((rows, width), F32),
        in_specs=[hbm, hbm, pl.BlockSpec(memory_space=pltpu.SMEM), vmem, hbm],
        out_specs=vmem,
        scratch_shapes=[scratch],
        compiler_params=pltpu.CompilerParams(
            collective_id=0, has_side_effects=True, vmem_limit_bytes=50 * 2**20
        ),
    )(lower, upper, jnp.swapaxes(tile_mask, 1, 2), row_map, schur)
    return front + added


def solution(mesh):
    count, cols = mesh.shape["row"], mesh.shape["col"]
    split = P(None, "row", "col")
    return jax.shard_map(
        functools.partial(shards, count, cols),
        mesh=mesh,
        in_specs=(split, split, split, split, P(None, "row"), P("row", "col")),
        out_specs=P("row", "col"),
        check_vma=False,
    )
```

```python
import functools

import jax
import jax.numpy as jnp
from jax import lax
from jax.experimental import pallas as pl
from jax.experimental.pallas import tpu as pltpu
from jax.sharding import PartitionSpec as P

TILE = 128
X = 4
CORES = 2
STEPS = ((0, 0, 1), (0, 1, 1), (0, 2, 2), (1, 0, 2), (1, 2, 2))
DIRECT = 2
GROUPS = (1, 1, 1, 1, 4)
MESH = pl.DeviceIdType.MESH
F32 = jnp.float32
BF16 = jnp.bfloat16
I32 = jnp.int32


def dot(a, b):
    return jnp.dot(a, b, preferred_element_type=F32)


def iota(shape, dim):
    return lax.broadcasted_iota(I32, shape, dim)


def kernel(
    dims,
    lower_hbm,
    upper_hbm,
    mask_ref,
    map_ref,
    schur_hbm,
    out_ref,
    s,
):
    count, cols, rows, width, depth, cap = dims
    zs = count // X
    ys = cols // CORES
    quarter = width // 4
    slots = count * cap
    steps = len(STEPS)
    me = lax.axis_index("row")
    col = lax.axis_index("col")
    my_z = me // X
    my_x = lax.rem(me, X)
    my_y = col // CORES
    core = lax.rem(col, CORES)
    partner = my_y * CORES + (1 - core)
    lower, upper, schur, packed, wide, panel = s["lower"], s["upper"], s["schur"], s["packed"], s["wide"], s["panel"]
    square, hot, owner = s["square"], s["hot"], s["owner"]
    rows_info, cols_info, place_info = s["rows_info"], s["cols_info"], s["place_info"]
    scale_col, both, both_in = s["scale_col"], s["both"], s["both_in"]
    code_out, code_in, meta_out, meta_in = s["code_out"], s["code_in"], s["meta_out"], s["meta_in"]
    meta_flat, spread = s["meta_flat"], s["spread"]
    local_sem = s["local_sem"]

    barrier = pltpu.get_barrier_semaphore()

    def greet_row(k, carry):
        pl.semaphore_signal(barrier, inc=1, device_id=(lax.rem(me + k, count), col), device_id_type=MESH)
        return carry

    def greet_col(k, carry):
        pl.semaphore_signal(barrier, inc=1, device_id=(me, lax.rem(col + k, cols)), device_id_type=MESH)
        return carry

    lax.fori_loop(1, count, greet_row, 0)
    lax.fori_loop(1, cols, greet_col, 0)

    lower_copy = pltpu.make_async_copy(lower_hbm, lower, local_sem.at[1])
    upper_copy = pltpu.make_async_copy(upper_hbm, upper, local_sem.at[2])
    schur_copy = pltpu.make_async_copy(schur_hbm, schur, local_sem.at[0])
    lower_copy.start()
    upper_copy.start()
    schur_copy.start()

    def remote(source, target, sent, got, device):
        return pltpu.make_async_remote_copy(
            src_ref=source, dst_ref=target, send_sem=sent, recv_sem=got, device_id=device, device_id_type=MESH
        )

    def total(ref, sent, got):
        return remote(ref, ref, sent, got, (me, partner))

    def pack(child):
        for tile in range(rows // TILE):
            at = pl.ds(tile * TILE, TILE)
            second = mask_ref[child, 1, tile]
            packed[child, col, at, :] = jnp.where(
                second == 1, lower[child, at, TILE : 2 * TILE], lower[child, at, 0:TILE]
            )
        row = iota((16, TILE), 0)
        flags = jnp.zeros((16, TILE), F32)
        for tile in range(rows // TILE):
            flags = jnp.where(row == tile, mask_ref[child, 1, tile].astype(F32), flags)
        packed[child, col, pl.ds(rows, 16), :] = flags.astype(BF16)

    def upper_block(step):
        child, first, number = STEPS[step]
        return upper.at[child, :, pl.ds(first * quarter, number * quarter)]

    def panel_block(step, z, x):
        start = pl.multiple_of((z * X + x) * depth, depth)
        return panel[step].at[pl.ds(start, depth), :]

    def nearest(n):
        half = n // 2 + 1
        return half + lax.rem(n, 2) * (zs - 2 * half)

    def z_copy(step, dz):
        z = lax.rem(my_z + dz, zs)
        return remote(
            upper_block(step),
            panel_block(step, my_z, my_x),
            s["z_send"].at[step],
            s["z_recv"].at[step, dz],
            (z * X + my_x, col),
        )

    def behind(i):
        return nearest(i - 1) if i else 0

    def x_copy(step, i, way):
        z = lax.rem(my_z - behind(i) + zs, zs)
        return remote(
            upper_block(step) if i == 0 else panel_block(step, z, my_x),
            panel_block(step, z, my_x),
            s["x_send"].at[step],
            s["x_recv"].at[step, (1 + way) // 2, i % 2],
            (my_z * X + lax.rem(my_x + way + X, X), col),
        )

    def far_copy(step, i, way):
        z = lax.rem(my_z - behind(i) + zs, zs)
        block = panel_block(step, z, lax.rem(my_x - way + X, X))
        return remote(
            block,
            block,
            s["x_send"].at[step],
            s["far_recv"].at[step],
            (my_z * X + lax.rem(my_x + way + X, X), col),
        )

    def send_own(step):
        for way in (1, -1):
            x_copy(step, 0, way).start()
        pltpu.make_async_copy(upper_block(step), panel_block(step, my_z, my_x), local_sem.at[3 + step]).start()

    def send_upper(step):
        def body(n, carry):
            z_copy(step, nearest(n)).start()
            return carry

        lax.fori_loop(0, zs - 1, body, 0)
        send_own(step)

    def pass_upper(step):
        for i in range(1, zs):
            z_copy(step, behind(i)).wait_recv()
            for way in (1, -1):
                x_copy(step, i, way).start()

    def near_x(step, way, part):
        return total(
            panel[step].at[pl.ds(0, zs // 2 * depth), :],
            s["x_send"].at[step],
            s["x_recv"].at[step, (1 + way) // 2, part],
        )

    def x_far(step):
        for way, part in ((1, 0), (-1, 1)):
            near_x(step, way, part).wait_recv()
            for i in range(part, zs, 2):
                far_copy(step, i, way).start()

    def reach(step, way):
        return zs // 2 if (step % 2 == 0) == (way > 0) else zs // 2 - 1

    def hop_copy(step, way, hop):
        z = lax.rem(my_z - way * (hop - 1) + zs, zs)
        block = upper_block(step) if hop == 1 else panel_block(step, z, my_x)
        return remote(
            block,
            panel_block(step, z, my_x),
            s["z_send"].at[step],
            s["z_recv"].at[step, (way * hop) % zs],
            (lax.rem(my_z + way + zs, zs) * X + my_x, col),
        )

    def hop_wait(step, hop):
        for way in (1, -1):
            if hop <= reach(step, way):
                hop_copy(step, way, hop).wait_recv()

    def hop_send(step, hop):
        for way in (1, -1):
            if hop <= reach(step, way):
                hop_copy(step, way, hop).start()

    def hops(hop):
        for step in range(DIRECT, steps):
            hop_wait(step, hop)
            hop_send(step, hop + 1)

    def x_spread(step):
        send_own(step)
        for i in range(1, zs):
            for way in (1, -1):
                x_copy(step, i, way).start()

    def all_x(step):
        return total(
            panel[step].at[pl.ds(0, (X - 1) * zs * depth), :], s["x_send"].at[step], s["far_recv"].at[step]
        )

    def wait_upper(step):
        pltpu.make_async_copy(upper_block(step), panel_block(step, my_z, my_x), local_sem.at[3 + step]).wait()
        near_x(step, 1, 1).wait_recv()
        near_x(step, -1, 0).wait_recv()
        total(
            panel[step].at[pl.ds(0, zs * depth), :], s["x_send"].at[step], s["far_recv"].at[step]
        ).wait_recv()

    middle = rows // 2
    parts = (pl.ds(0, middle), pl.ds(middle, rows + 16 - middle))

    def y_copy(child, way, part, hop):
        block = lax.rem(my_y - way * (hop - 1) + ys, ys) * CORES + core
        ref = packed.at[child, block, parts[part], :]
        return remote(
            ref,
            ref,
            s["y_send"].at[child, (1 + way) // 2, part, hop - 1],
            s["y_recv"].at[child, (1 + way) // 2, part, hop - 1],
            (me, lax.rem(my_y + way + ys, ys) * CORES + core),
        )

    def c_copy(child, behind, part):
        block = lax.rem(my_y - behind + ys, ys) * CORES + core
        ref = packed.at[child, block, parts[part], :]
        return remote(ref, ref, s["c_send"].at[child], s["c_recv"].at[child], (me, partner))

    def send_lower(child):
        for way, part in ((1, 0), (-1, 1), (1, 1), (-1, 0)):
            y_copy(child, way, part, 1).start()
        for part in range(2):
            c_copy(child, 0, part).start()

    def pass_lower(child):
        for way, part in ((1, 0), (-1, 1)):
            y_copy(child, way, part, 1).wait_recv()
            y_copy(child, way, part, 2).start()
            c_copy(child, way, part).start()

    def pass_lower_again(child):
        for way, part in ((1, 1), (-1, 0)):
            y_copy(child, way, part, 1).wait_recv()
            c_copy(child, way, part).start()
        for way, part in ((1, 0), (-1, 1)):
            y_copy(child, way, part, 2).wait_recv()
            c_copy(child, 2 * way, part).start()

    def all_c(child):
        return total(packed.at[child, pl.ds(0, ys)], s["c_send"].at[child], s["c_recv"].at[child])

    def index_rows():
        def strict(b, carry):
            at = pl.ds(pl.multiple_of(b * TILE, TILE), TILE)
            before = iota((TILE, rows), 0) + b * TILE < iota((TILE, rows), 1)
            square[at, :] = jnp.where(before, 1.0, 0.0).astype(BF16)
            return carry

        lax.fori_loop(0, rows // TILE, strict, 0)
        for child in range(2):
            line = map_ref[pl.ds(child, 1), :]
            same = iota((count, rows), 0) == line // rows
            owner[child] = jnp.where(same, 1.0, 0.0).astype(BF16)
        rows_info[...] = jnp.zeros_like(rows_info)
        for child in range(2):
            line = map_ref[pl.ds(child, 1), :]
            hits = owner[child]
            ahead = dot(hits, square[...])
            rank = jnp.sum(ahead * hits.astype(F32), axis=0, keepdims=True)
            spot = lax.rem(line, rows) + 1
            rows_info[pl.ds(4 * child, 1), :] = rank
            rows_info[pl.ds(4 * child + 1, 1), :] = (spot // 32).astype(F32)
            rows_info[pl.ds(4 * child + 2, 1), :] = lax.rem(spot, 32).astype(F32)
            rows_info[pl.ds(4 * child + 3, 1), :] = (line // rows).astype(F32)

    def index_cols():
        def identity(b, carry):
            at = pl.ds(pl.multiple_of(b * TILE, TILE), TILE)
            equal = iota((TILE, rows), 0) + b * TILE == iota((TILE, rows), 1)
            square[at, :] = jnp.where(equal, 1.0, 0.0).astype(BF16)
            return carry

        lax.fori_loop(0, rows // TILE, identity, 0)
        cols_info[...] = lax.dot_general(
            square[...], rows_info[...].astype(BF16), (((1,), (1,)), ((), ())), preferred_element_type=F32
        )
        for child in range(2):
            lane = iota((rows, TILE), 1).astype(F32)
            match = lane - 64.0 == cols_info[:, 4 * child : 4 * child + 1]
            tops = jnp.where(match, cols_info[:, 4 * child + 1 : 4 * child + 2], 0.0).astype(BF16)
            ends = jnp.where(match, cols_info[:, 4 * child + 2 : 4 * child + 3], 0.0).astype(BF16)
            place_info[child] = 32.0 * dot(owner[child], tops) + dot(owner[child], ends)
        slot = iota((TILE, slots), 1).astype(F32)
        inner = slot - cap * jnp.floor((slot + 0.5) * (1.0 / cap))
        lane = iota((TILE, slots), 0).astype(F32)
        spread[0] = jnp.where(lane == inner, 1.0, 0.0).astype(BF16)
        spread[1] = jnp.where(lane - 64.0 == inner, 1.0, 0.0).astype(BF16)

    def build_hot(child):
        flat = rows_info[pl.ds(4 * child + 3, 1), :] * float(cap) + rows_info[pl.ds(4 * child, 1), :]

        def body(b, carry):
            at = pl.ds(pl.multiple_of(b * TILE, TILE), TILE)
            slot = (iota((TILE, rows), 0) + b * TILE).astype(F32)
            hot[at, :] = jnp.where(slot == flat, 1.0, 0.0).astype(BF16)
            return carry

        lax.fori_loop(0, slots // TILE, body, 0)

    def widen(child):
        def body(j, carry):
            flags = packed[child, j, pl.ds(rows, 16), :].astype(F32)
            for tile in range(rows // TILE):
                at = pl.ds(tile * TILE, TILE)
                block = packed[child, j, at, :].astype(F32)
                flag = flags[tile : tile + 1, :]
                left = pl.multiple_of(j * 2 * TILE, TILE)
                right = pl.multiple_of(j * 2 * TILE + TILE, TILE)
                wide[at, pl.ds(left, TILE)] = (block * (1.0 - flag)).astype(BF16)
                wide[at, pl.ds(right, TILE)] = (block * flag).astype(BF16)
            return carry

        lax.fori_loop(0, cols, body, 0)

    def contribute(step):
        child, first, number = STEPS[step]
        cw = number * quarter
        part = rows // 2
        for b in range(2):
            at = pl.ds(b * part, part)
            update = dot(wide[at, :], panel[step][...])
            value = schur[child, at, pl.ds(first * quarter, cw)] - update
            peak = jnp.maximum(jnp.max(jnp.abs(value), axis=1, keepdims=True), 1e-30)
            scale_col[at, :] = jnp.broadcast_to(peak * ((1.0 + 2.0**-8) / 32767.0), (part, TILE)).astype(BF16)
            inverse = 1.0 / scale_col[at, :].astype(F32)
            code = jnp.floor(value * inverse[:, 0:1] + 0.5)
            top = jnp.floor(code * (1.0 / 256.0))
            both[at, 0:cw] = top.astype(BF16)
            both[at, cw : 2 * cw] = (code - 256.0 * top).astype(BF16)
        size = slots // 3
        for b in range(3):
            at = pl.ds(b * size, size)
            moved = dot(hot[at, :], both[:, 0 : 2 * cw])
            code = 256.0 * moved[:, 0:cw] + moved[:, cw : 2 * cw]
            code_out[step][at, :] = code.astype(I32).astype(jnp.int16)
        lane = iota((rows, TILE), 1).astype(F32)
        match = lane == cols_info[:, 4 * child : 4 * child + 1]
        scales = jnp.where(match, scale_col[...].astype(F32), 0.0).astype(BF16)
        meta = dot(owner[child], scales) + place_info[child]
        for t in range(count):
            meta_out[step, t] = meta[t : t + 1, :]

    def rows_of(t):
        return pl.ds(pl.multiple_of(t * cap, 16), cap)

    def shift(n):
        place = n // 2 + lax.rem(n, 2) * (count - 2 - 2 * (n // 2))
        half = place // 2 + 1
        return half + lax.rem(place, 2) * (count - 2 * half)

    def e_copy(step, n, group):
        t = lax.rem(me + shift(n), count)
        return remote(
            code_out[step].at[rows_of(t), :],
            code_in[step].at[rows_of(n), :],
            s["e_send"].at[step],
            s["e_recv"].at[step, group],
            (t, col),
        )

    def m_copy(step, n, group):
        t = lax.rem(me + shift(n), count)
        return remote(
            meta_out.at[step, t], meta_in.at[step, n], s["m_send"].at[step], s["m_recv"].at[step, group], (t, col)
        )

    def own_copies(step):
        return (
            pltpu.make_async_copy(
                code_out[step].at[rows_of(me), :], code_in[step].at[rows_of(count - 1), :], local_sem.at[8 + step]
            ),
            pltpu.make_async_copy(meta_out.at[step, me], meta_in.at[step, count - 1], local_sem.at[13 + step]),
        )

    def exchange(step):
        members = count // GROUPS[step]
        for group in range(GROUPS[step]):

            def body(n, carry):
                m_copy(step, n, group).start()
                e_copy(step, n, group).start()
                return carry

            lax.fori_loop(group * members, min((group + 1) * members, count - 1), body, 0)
        for copy in own_copies(step):
            copy.start()

    def all_codes(step, group, number):
        ref = code_in[step].at[pl.ds(0, number * cap), :]
        return total(ref, s["e_send"].at[step], s["e_recv"].at[step, group])

    def all_meta(step, group, number):
        ref = meta_in.at[step, pl.ds(0, number)]
        return total(ref, s["m_send"].at[step], s["m_recv"].at[step, group])

    def collect(step, group):
        _, first, number = STEPS[step]
        cw = number * quarter
        members = count // GROUPS[step]
        others = members
        if group == GROUPS[step] - 1:
            others = members - 1
            for copy in own_copies(step):
                copy.wait()
        all_meta(step, group, others).wait_recv()
        for m in range(members):
            meta_flat[m : m + 1, :] = meta_in[step, group * members + m]
        flat = meta_flat[0:members, :]
        tops = jnp.floor(flat * (1.0 / 32.0))
        ends = flat - 32.0 * tops
        size = members * cap
        for_place, for_scale = spread[1, :, 0:size], spread[0, :, 0:size]
        places = 32.0 * dot(tops.astype(BF16), for_place) + dot(ends.astype(BF16), for_place)
        scales = dot(flat.astype(BF16), for_scale)
        slot = iota((members, size), 1)
        start = iota((members, size), 0) * cap
        own = (slot >= start) & (slot < start + cap)
        place = jnp.sum(jnp.where(own, places, 0.0), axis=0, keepdims=True)
        scale = jnp.sum(jnp.where(own, scales, 0.0), axis=0, keepdims=True)
        all_codes(step, group, others).wait_recv()
        code = code_in[step][group * size : (group + 1) * size, :].astype(I32)
        both_in[0:size, 0:cw] = (code >> 8).astype(F32).astype(BF16)
        both_in[0:size, cw : 2 * cw] = (code & 255).astype(F32).astype(BF16)
        part = rows // 2
        for b in range(2):
            target = (iota((part, size), 0) + (b * part + 1)).astype(F32)
            pick = jnp.where(target == place, scale, 0.0).astype(BF16)
            at = (pl.ds(b * part, part), pl.ds(first * quarter, cw))
            moved = dot(pick, both_in[0:size, 0 : 2 * cw])
            value = 256.0 * moved[:, 0:cw] + moved[:, cw : 2 * cw]
            if STEPS[step][0] == 0 and group == 0:
                out_ref[at] = value
            else:
                out_ref[at] = out_ref[at] + value

    lower_copy.wait()
    upper_copy.wait()
    pack(0)
    index_rows()
    pl.semaphore_wait(barrier, count + cols - 2)
    send_upper(0)
    send_lower(0)
    send_upper(1)
    for step in range(DIRECT, steps):
        hop_send(step, 1)
    pack(1)
    index_cols()
    pass_upper(0)
    pass_lower(0)
    hops(1)
    pass_upper(1)
    x_far(0)
    pass_lower_again(0)
    send_lower(1)
    hops(2)
    build_hot(0)
    x_far(1)
    hops(3)
    all_c(0).wait_recv()
    widen(0)
    schur_copy.wait()
    wait_upper(0)
    contribute(0)
    for step in range(DIRECT, steps):
        hop_wait(step, 4)
    x_spread(2)
    exchange(0)
    pass_lower(1)
    wait_upper(1)
    contribute(1)
    exchange(1)
    x_far(2)
    x_spread(3)
    pass_lower_again(1)
    wait_upper(2)
    contribute(2)
    exchange(2)
    all_c(1).wait_recv()
    widen(1)
    build_hot(1)
    x_far(3)
    x_spread(4)
    collect(0, 0)
    wait_upper(3)
    contribute(3)
    exchange(3)
    x_far(4)
    collect(1, 0)
    wait_upper(4)
    contribute(4)
    exchange(4)
    for step in range(2, steps):
        for group in range(GROUPS[step]):
            collect(step, group)

    for step in range(steps):
        total(
            panel[step].at[pl.ds(0, (zs - 1) * depth), :], s["z_send"].at[step], s["z_recv"].at[step, 0]
        ).wait_send()
        all_x(step).wait_send()
        all_codes(step, 0, count - 1).wait_send()
        all_meta(step, 0, count - 1).wait_send()
    for child in range(2):
        for part in range(2):
            for way in (1, -1):
                y_copy(child, way, part, 1).wait_send()
            y_copy(child, 1 - 2 * part, part, 2).wait_send()
        all_c(child).wait_send()


def shards(count, cols, schur, lower, upper, tile_mask, row_map, front):
    children, rows, _ = lower.shape
    width = schur.shape[2]
    depth = upper.shape[1]
    cap = 3 * rows // (2 * count)
    slots = count * cap
    steps = len(STEPS)
    full = depth * count
    zs = count // X
    dims = (count, cols, rows, width, depth, cap)
    widths = [width // 4 * number for _, _, number in STEPS]
    half = width // 2
    vmem = pl.BlockSpec(memory_space=pltpu.VMEM)
    hbm = pl.BlockSpec(memory_space=pltpu.HBM)
    dma = pltpu.SemaphoreType.DMA
    scratch = dict(
        lower=pltpu.VMEM(lower.shape, BF16),
        upper=pltpu.VMEM(upper.shape, BF16),
        schur=pltpu.VMEM(schur.shape, F32),
        packed=pltpu.VMEM((children, cols, rows + 16, TILE), BF16),
        wide=pltpu.VMEM((rows, full), BF16),
        panel=[pltpu.VMEM((full, w), BF16) for w in widths],
        square=pltpu.VMEM((rows, rows), BF16),
        hot=pltpu.VMEM((slots, rows), BF16),
        owner=pltpu.VMEM((children, count, rows), BF16),
        rows_info=pltpu.VMEM((8, rows), F32),
        cols_info=pltpu.VMEM((rows, 8), F32),
        place_info=pltpu.VMEM((children, count, TILE), F32),
        scale_col=pltpu.VMEM((rows, TILE), BF16),
        both=pltpu.VMEM((rows, 2 * half), BF16),
        code_out=[pltpu.VMEM((slots, w), jnp.int16) for w in widths],
        code_in=[pltpu.VMEM((slots, w), jnp.int16) for w in widths],
        meta_out=pltpu.VMEM((steps, count, 1, TILE), F32),
        meta_in=pltpu.VMEM((steps, count, 1, TILE), F32),
        meta_flat=pltpu.VMEM((count, TILE), F32),
        spread=pltpu.VMEM((2, TILE, slots), BF16),
        both_in=pltpu.VMEM((slots, 2 * half), BF16),
        local_sem=dma((18,)),
        z_send=dma((steps,)),
        z_recv=dma((steps, zs)),
        x_send=dma((steps,)),
        x_recv=dma((steps, 2, 2)),
        far_recv=dma((steps,)),
        y_send=dma((children, 2, 2, 2)),
        y_recv=dma((children, 2, 2, 2)),
        c_send=dma((children,)),
        c_recv=dma((children,)),
        e_send=dma((steps,)),
        e_recv=dma((steps, max(GROUPS))),
        m_send=dma((steps,)),
        m_recv=dma((steps, max(GROUPS))),
    )
    added = pl.pallas_call(
        functools.partial(kernel, dims),
        out_shape=jax.ShapeDtypeStruct((rows, width), F32),
        in_specs=[hbm, hbm, pl.BlockSpec(memory_space=pltpu.SMEM), vmem, hbm],
        out_specs=vmem,
        scratch_shapes=[scratch],
        compiler_params=pltpu.CompilerParams(
            collective_id=0, has_side_effects=True, vmem_limit_bytes=50 * 2**20
        ),
    )(
        pltpu.with_memory_space_constraint(lower, pltpu.HBM),
        pltpu.with_memory_space_constraint(upper, pltpu.HBM),
        jnp.swapaxes(tile_mask, 1, 2),
        pltpu.with_memory_space_constraint(row_map, pltpu.HBM),
        schur,
    )
    return front + added


def solution(mesh):
    count, cols = mesh.shape["row"], mesh.shape["col"]
    split = P(None, "row", "col")
    return jax.shard_map(
        functools.partial(shards, count, cols),
        mesh=mesh,
        in_specs=(split, split, split, split, P(None, "row"), P("row", "col")),
        out_specs=P("row", "col"),
        check_vma=False,
    )
```

```python
import functools

import jax
import jax.numpy as jnp
from jax import lax
from jax.experimental import pallas as pl
from jax.experimental.pallas import tpu as pltpu
from jax.sharding import PartitionSpec as P

TILE = 128
X = 4
CORES = 2
STEPS = ((0, 0, 1), (0, 1, 1), (0, 2, 2), (1, 0, 2), (1, 2, 2))
DIRECT = 2
GROUPS = (1, 1, 1, 1, 4)
MESH = pl.DeviceIdType.MESH
F32 = jnp.float32
BF16 = jnp.bfloat16
I32 = jnp.int32


def dot(a, b):
    return jnp.dot(a, b, preferred_element_type=F32)


def iota(shape, dim):
    return lax.broadcasted_iota(I32, shape, dim)


def kernel(
    dims,
    lower_hbm,
    upper_hbm,
    mask_ref,
    map_ref,
    schur_hbm,
    out_ref,
    s,
):
    count, cols, rows, width, depth, cap = dims
    zs = count // X
    ys = cols // CORES
    quarter = width // 4
    slots = count * cap
    steps = len(STEPS)
    me = lax.axis_index("row")
    col = lax.axis_index("col")
    my_z = me // X
    my_x = lax.rem(me, X)
    my_y = col // CORES
    core = lax.rem(col, CORES)
    partner = my_y * CORES + (1 - core)
    lower, upper, schur, packed, wide, panel = s["lower"], s["upper"], s["schur"], s["packed"], s["wide"], s["panel"]
    square, hot, owner = s["square"], s["hot"], s["owner"]
    rows_info, cols_info, place_info = s["rows_info"], s["cols_info"], s["place_info"]
    scale_col, both, both_in = s["scale_col"], s["both"], s["both_in"]
    code_out, code_in, meta_out, meta_in = s["code_out"], s["code_in"], s["meta_out"], s["meta_in"]
    meta_flat, spread = s["meta_flat"], s["spread"]
    local_sem = s["local_sem"]

    barrier = pltpu.get_barrier_semaphore()

    def greet_row(k, carry):
        pl.semaphore_signal(barrier, inc=1, device_id=(lax.rem(me + k, count), col), device_id_type=MESH)
        return carry

    def greet_col(k, carry):
        pl.semaphore_signal(barrier, inc=1, device_id=(me, lax.rem(col + k, cols)), device_id_type=MESH)
        return carry

    lax.fori_loop(1, count, greet_row, 0)
    lax.fori_loop(1, cols, greet_col, 0)

    lower_copy = pltpu.make_async_copy(lower_hbm, lower, local_sem.at[1])
    upper_copy = pltpu.make_async_copy(upper_hbm, upper, local_sem.at[2])
    schur_copy = pltpu.make_async_copy(schur_hbm, schur, local_sem.at[0])
    lower_copy.start()
    upper_copy.start()
    schur_copy.start()

    def remote(source, target, sent, got, device):
        return pltpu.make_async_remote_copy(
            src_ref=source, dst_ref=target, send_sem=sent, recv_sem=got, device_id=device, device_id_type=MESH
        )

    def total(ref, sent, got):
        return remote(ref, ref, sent, got, (me, partner))

    def pack(child):
        for tile in range(rows // TILE):
            at = pl.ds(tile * TILE, TILE)
            second = mask_ref[child, 1, tile]
            packed[child, col, at, :] = jnp.where(
                second == 1, lower[child, at, TILE : 2 * TILE], lower[child, at, 0:TILE]
            )
        row = iota((16, TILE), 0)
        flags = jnp.zeros((16, TILE), F32)
        for tile in range(rows // TILE):
            flags = jnp.where(row == tile, mask_ref[child, 1, tile].astype(F32), flags)
        packed[child, col, pl.ds(rows, 16), :] = flags.astype(BF16)

    def upper_block(step):
        child, first, number = STEPS[step]
        return upper.at[child, :, pl.ds(first * quarter, number * quarter)]

    def panel_block(step, z, x):
        start = pl.multiple_of((z * X + x) * depth, depth)
        return panel[step].at[pl.ds(start, depth), :]

    def nearest(n):
        half = n // 2 + 1
        return half + lax.rem(n, 2) * (zs - 2 * half)

    def z_copy(step, dz):
        z = lax.rem(my_z + dz, zs)
        return remote(
            upper_block(step),
            panel_block(step, my_z, my_x),
            s["z_send"].at[step],
            s["z_recv"].at[step, dz],
            (z * X + my_x, col),
        )

    def behind(i):
        return nearest(i - 1) if i else 0

    def x_copy(step, i, way):
        z = lax.rem(my_z - behind(i) + zs, zs)
        return remote(
            upper_block(step) if i == 0 else panel_block(step, z, my_x),
            panel_block(step, z, my_x),
            s["x_send"].at[step],
            s["x_recv"].at[step, (1 + way) // 2, i % 2],
            (my_z * X + lax.rem(my_x + way + X, X), col),
        )

    def far_copy(step, i, way):
        z = lax.rem(my_z - behind(i) + zs, zs)
        block = panel_block(step, z, lax.rem(my_x - way + X, X))
        return remote(
            block,
            block,
            s["x_send"].at[step],
            s["far_recv"].at[step],
            (my_z * X + lax.rem(my_x + way + X, X), col),
        )

    def send_own(step):
        for way in (1, -1):
            x_copy(step, 0, way).start()
        pltpu.make_async_copy(upper_block(step), panel_block(step, my_z, my_x), local_sem.at[3 + step]).start()

    def send_upper(step):
        def body(n, carry):
            z_copy(step, nearest(n)).start()
            return carry

        lax.fori_loop(0, zs - 1, body, 0)
        send_own(step)

    def pass_upper(step):
        for i in range(1, zs):
            z_copy(step, behind(i)).wait_recv()
            for way in (1, -1):
                x_copy(step, i, way).start()

    def near_x(step, way, part):
        return total(
            panel[step].at[pl.ds(0, zs // 2 * depth), :],
            s["x_send"].at[step],
            s["x_recv"].at[step, (1 + way) // 2, part],
        )

    def x_far(step):
        for way, part in ((1, 0), (-1, 1)):
            near_x(step, way, part).wait_recv()
            for i in range(part, zs, 2):
                far_copy(step, i, way).start()

    def reach(step, way):
        return zs // 2 if (step % 2 == 0) == (way > 0) else zs // 2 - 1

    def hop_copy(step, way, hop):
        z = lax.rem(my_z - way * (hop - 1) + zs, zs)
        block = upper_block(step) if hop == 1 else panel_block(step, z, my_x)
        return remote(
            block,
            panel_block(step, z, my_x),
            s["z_send"].at[step],
            s["z_recv"].at[step, (way * hop) % zs],
            (lax.rem(my_z + way + zs, zs) * X + my_x, col),
        )

    def hop_wait(step, hop):
        for way in (1, -1):
            if hop <= reach(step, way):
                hop_copy(step, way, hop).wait_recv()

    def hop_send(step, hop):
        for way in (1, -1):
            if hop <= reach(step, way):
                hop_copy(step, way, hop).start()

    def hops(hop):
        for step in range(DIRECT, steps):
            hop_wait(step, hop)
            hop_send(step, hop + 1)

    def x_spread(step):
        send_own(step)
        for i in range(1, zs):
            for way in (1, -1):
                x_copy(step, i, way).start()

    def all_x(step):
        return total(
            panel[step].at[pl.ds(0, (X - 1) * zs * depth), :], s["x_send"].at[step], s["far_recv"].at[step]
        )

    def wait_upper(step):
        pltpu.make_async_copy(upper_block(step), panel_block(step, my_z, my_x), local_sem.at[3 + step]).wait()
        near_x(step, 1, 1).wait_recv()
        near_x(step, -1, 0).wait_recv()
        total(
            panel[step].at[pl.ds(0, zs * depth), :], s["x_send"].at[step], s["far_recv"].at[step]
        ).wait_recv()

    middle = rows // 2
    parts = (pl.ds(0, middle), pl.ds(middle, rows + 16 - middle))

    def y_copy(child, way, part, hop):
        block = lax.rem(my_y - way * (hop - 1) + ys, ys) * CORES + core
        ref = packed.at[child, block, parts[part], :]
        return remote(
            ref,
            ref,
            s["y_send"].at[child, (1 + way) // 2, part, hop - 1],
            s["y_recv"].at[child, (1 + way) // 2, part, hop - 1],
            (me, lax.rem(my_y + way + ys, ys) * CORES + core),
        )

    def c_copy(child, behind, part):
        block = lax.rem(my_y - behind + ys, ys) * CORES + core
        ref = packed.at[child, block, parts[part], :]
        return remote(ref, ref, s["c_send"].at[child], s["c_recv"].at[child], (me, partner))

    def send_lower(child):
        for way, part in ((1, 0), (-1, 1), (1, 1), (-1, 0)):
            y_copy(child, way, part, 1).start()
        for part in range(2):
            c_copy(child, 0, part).start()

    def pass_lower(child):
        for way, part in ((1, 0), (-1, 1)):
            y_copy(child, way, part, 1).wait_recv()
            y_copy(child, way, part, 2).start()
            c_copy(child, way, part).start()

    def pass_lower_again(child):
        for way, part in ((1, 1), (-1, 0)):
            y_copy(child, way, part, 1).wait_recv()
            c_copy(child, way, part).start()
        for way, part in ((1, 0), (-1, 1)):
            y_copy(child, way, part, 2).wait_recv()
            c_copy(child, 2 * way, part).start()

    def all_c(child):
        return total(packed.at[child, pl.ds(0, ys)], s["c_send"].at[child], s["c_recv"].at[child])

    def index_rows():
        def strict(b, carry):
            at = pl.ds(pl.multiple_of(b * TILE, TILE), TILE)
            before = iota((TILE, rows), 0) + b * TILE < iota((TILE, rows), 1)
            square[at, :] = jnp.where(before, 1.0, 0.0).astype(BF16)
            return carry

        lax.fori_loop(0, rows // TILE, strict, 0)
        for child in range(2):
            line = map_ref[pl.ds(child, 1), :]
            same = iota((count, rows), 0) == line // rows
            owner[child] = jnp.where(same, 1.0, 0.0).astype(BF16)
        rows_info[...] = jnp.zeros_like(rows_info)
        for child in range(2):
            line = map_ref[pl.ds(child, 1), :]
            hits = owner[child]
            ahead = dot(hits, square[...])
            rank = jnp.sum(ahead * hits.astype(F32), axis=0, keepdims=True)
            spot = lax.rem(line, rows) + 1
            rows_info[pl.ds(4 * child, 1), :] = rank
            rows_info[pl.ds(4 * child + 1, 1), :] = (spot // 32).astype(F32)
            rows_info[pl.ds(4 * child + 2, 1), :] = lax.rem(spot, 32).astype(F32)
            rows_info[pl.ds(4 * child + 3, 1), :] = (line // rows).astype(F32)

    def index_cols():
        def identity(b, carry):
            at = pl.ds(pl.multiple_of(b * TILE, TILE), TILE)
            equal = iota((TILE, rows), 0) + b * TILE == iota((TILE, rows), 1)
            square[at, :] = jnp.where(equal, 1.0, 0.0).astype(BF16)
            return carry

        lax.fori_loop(0, rows // TILE, identity, 0)
        cols_info[...] = lax.dot_general(
            square[...], rows_info[...].astype(BF16), (((1,), (1,)), ((), ())), preferred_element_type=F32
        )
        for child in range(2):
            lane = iota((rows, TILE), 1).astype(F32)
            match = lane - 64.0 == cols_info[:, 4 * child : 4 * child + 1]
            tops = jnp.where(match, cols_info[:, 4 * child + 1 : 4 * child + 2], 0.0).astype(BF16)
            ends = jnp.where(match, cols_info[:, 4 * child + 2 : 4 * child + 3], 0.0).astype(BF16)
            place_info[child] = 32.0 * dot(owner[child], tops) + dot(owner[child], ends)
        slot = iota((TILE, slots), 1).astype(F32)
        inner = slot - cap * jnp.floor((slot + 0.5) * (1.0 / cap))
        lane = iota((TILE, slots), 0).astype(F32)
        spread[0] = jnp.where(lane == inner, 1.0, 0.0).astype(BF16)
        spread[1] = jnp.where(lane - 64.0 == inner, 1.0, 0.0).astype(BF16)

    def build_hot(child):
        flat = rows_info[pl.ds(4 * child + 3, 1), :] * float(cap) + rows_info[pl.ds(4 * child, 1), :]

        def body(b, carry):
            at = pl.ds(pl.multiple_of(b * TILE, TILE), TILE)
            slot = (iota((TILE, rows), 0) + b * TILE).astype(F32)
            hot[at, :] = jnp.where(slot == flat, 1.0, 0.0).astype(BF16)
            return carry

        lax.fori_loop(0, slots // TILE, body, 0)

    def widen(child):
        def body(j, carry):
            flags = packed[child, j, pl.ds(rows, 16), :].astype(F32)
            for tile in range(rows // TILE):
                at = pl.ds(tile * TILE, TILE)
                block = packed[child, j, at, :].astype(F32)
                flag = flags[tile : tile + 1, :]
                left = pl.multiple_of(j * 2 * TILE, TILE)
                right = pl.multiple_of(j * 2 * TILE + TILE, TILE)
                wide[at, pl.ds(left, TILE)] = (block * (1.0 - flag)).astype(BF16)
                wide[at, pl.ds(right, TILE)] = (block * flag).astype(BF16)
            return carry

        lax.fori_loop(0, cols, body, 0)

    def contribute(step):
        child, first, number = STEPS[step]
        cw = number * quarter
        part = rows // 2
        for b in range(2):
            at = pl.ds(b * part, part)
            update = dot(wide[at, :], panel[step][...])
            value = schur[child, at, pl.ds(first * quarter, cw)] - update
            peak = jnp.maximum(jnp.max(jnp.abs(value), axis=1, keepdims=True), 1e-30)
            scale_col[at, :] = jnp.broadcast_to(peak * ((1.0 + 2.0**-8) / 32767.0), (part, TILE)).astype(BF16)
            inverse = 1.0 / scale_col[at, :].astype(F32)
            code = jnp.floor(value * inverse[:, 0:1] + 0.5)
            top = jnp.floor(code * (1.0 / 256.0))
            both[at, 0:cw] = top.astype(BF16)
            both[at, cw : 2 * cw] = (code - 256.0 * top).astype(BF16)
        size = slots // 3
        for b in range(3):
            at = pl.ds(b * size, size)
            moved = dot(hot[at, :], both[:, 0 : 2 * cw])
            code = 256.0 * moved[:, 0:cw] + moved[:, cw : 2 * cw]
            code_out[step][at, :] = code.astype(I32).astype(jnp.int16)
        lane = iota((rows, TILE), 1).astype(F32)
        match = lane == cols_info[:, 4 * child : 4 * child + 1]
        scales = jnp.where(match, scale_col[...].astype(F32), 0.0).astype(BF16)
        meta = dot(owner[child], scales) + place_info[child]
        for t in range(count):
            meta_out[step, t] = meta[t : t + 1, :]

    def rows_of(t):
        return pl.ds(pl.multiple_of(t * cap, 16), cap)

    def shift(n):
        place = n // 2 + lax.rem(n, 2) * (count - 2 - 2 * (n // 2))
        half = place // 2 + 1
        return half + lax.rem(place, 2) * (count - 2 * half)

    def e_copy(step, n, group):
        t = lax.rem(me + shift(n), count)
        return remote(
            code_out[step].at[rows_of(t), :],
            code_in[step].at[rows_of(n), :],
            s["e_send"].at[step],
            s["e_recv"].at[step, group],
            (t, col),
        )

    def m_copy(step, n, group):
        t = lax.rem(me + shift(n), count)
        return remote(
            meta_out.at[step, t], meta_in.at[step, n], s["m_send"].at[step], s["m_recv"].at[step, group], (t, col)
        )

    def own_copies(step):
        return (
            pltpu.make_async_copy(
                code_out[step].at[rows_of(me), :], code_in[step].at[rows_of(count - 1), :], local_sem.at[8 + step]
            ),
            pltpu.make_async_copy(meta_out.at[step, me], meta_in.at[step, count - 1], local_sem.at[13 + step]),
        )

    def exchange(step):
        members = count // GROUPS[step]
        for group in range(GROUPS[step]):

            def body(n, carry):
                m_copy(step, n, group).start()
                e_copy(step, n, group).start()
                return carry

            lax.fori_loop(group * members, min((group + 1) * members, count - 1), body, 0)
        for copy in own_copies(step):
            copy.start()

    def all_codes(step, group, number):
        ref = code_in[step].at[pl.ds(0, number * cap), :]
        return total(ref, s["e_send"].at[step], s["e_recv"].at[step, group])

    def all_meta(step, group, number):
        ref = meta_in.at[step, pl.ds(0, number)]
        return total(ref, s["m_send"].at[step], s["m_recv"].at[step, group])

    def collect(step, group):
        _, first, number = STEPS[step]
        cw = number * quarter
        members = count // GROUPS[step]
        others = members
        if group == GROUPS[step] - 1:
            others = members - 1
            for copy in own_copies(step):
                copy.wait()
        all_meta(step, group, others).wait_recv()
        for m in range(members):
            meta_flat[m : m + 1, :] = meta_in[step, group * members + m]
        flat = meta_flat[0:members, :]
        tops = jnp.floor(flat * (1.0 / 32.0))
        ends = flat - 32.0 * tops
        size = members * cap
        for_place, for_scale = spread[1, :, 0:size], spread[0, :, 0:size]
        places = 32.0 * dot(tops.astype(BF16), for_place) + dot(ends.astype(BF16), for_place)
        scales = dot(flat.astype(BF16), for_scale)
        slot = iota((members, size), 1)
        start = iota((members, size), 0) * cap
        own = (slot >= start) & (slot < start + cap)
        place = jnp.sum(jnp.where(own, places, 0.0), axis=0, keepdims=True)
        scale = jnp.sum(jnp.where(own, scales, 0.0), axis=0, keepdims=True)
        all_codes(step, group, others).wait_recv()
        code = code_in[step][group * size : (group + 1) * size, :].astype(I32)
        both_in[0:size, 0:cw] = (code >> 8).astype(F32).astype(BF16)
        both_in[0:size, cw : 2 * cw] = (code & 255).astype(F32).astype(BF16)
        part = rows // 2
        for b in range(2):
            target = (iota((part, size), 0) + (b * part + 1)).astype(F32)
            pick = jnp.where(target == place, scale, 0.0).astype(BF16)
            at = (pl.ds(b * part, part), pl.ds(first * quarter, cw))
            moved = dot(pick, both_in[0:size, 0 : 2 * cw])
            value = 256.0 * moved[:, 0:cw] + moved[:, cw : 2 * cw]
            if STEPS[step][0] == 0 and group == 0:
                out_ref[at] = value
            else:
                out_ref[at] = out_ref[at] + value

    lower_copy.wait()
    upper_copy.wait()
    pack(0)
    pl.semaphore_wait(barrier, count + cols - 2)
    send_upper(0)
    send_lower(0)
    send_upper(1)
    for step in range(DIRECT, steps):
        hop_send(step, 1)
    pack(1)
    index_rows()
    index_cols()
    pass_upper(0)
    pass_lower(0)
    hops(1)
    pass_upper(1)
    x_far(0)
    pass_lower_again(0)
    send_lower(1)
    hops(2)
    build_hot(0)
    x_far(1)
    hops(3)
    all_c(0).wait_recv()
    widen(0)
    schur_copy.wait()
    wait_upper(0)
    for step in range(DIRECT, steps):
        hop_wait(step, 4)
    x_spread(2)
    contribute(0)
    exchange(0)
    pass_lower(1)
    wait_upper(1)
    contribute(1)
    exchange(1)
    x_far(2)
    x_spread(3)
    pass_lower_again(1)
    wait_upper(2)
    contribute(2)
    exchange(2)
    all_c(1).wait_recv()
    widen(1)
    build_hot(1)
    x_far(3)
    x_spread(4)
    collect(0, 0)
    wait_upper(3)
    contribute(3)
    exchange(3)
    x_far(4)
    collect(1, 0)
    wait_upper(4)
    contribute(4)
    exchange(4)
    for step in range(2, steps):
        for group in range(GROUPS[step]):
            collect(step, group)

    for step in range(steps):
        total(
            panel[step].at[pl.ds(0, (zs - 1) * depth), :], s["z_send"].at[step], s["z_recv"].at[step, 0]
        ).wait_send()
        all_x(step).wait_send()
        all_codes(step, 0, count - 1).wait_send()
        all_meta(step, 0, count - 1).wait_send()
    for child in range(2):
        for part in range(2):
            for way in (1, -1):
                y_copy(child, way, part, 1).wait_send()
            y_copy(child, 1 - 2 * part, part, 2).wait_send()
        all_c(child).wait_send()


def shards(count, cols, schur, lower, upper, tile_mask, row_map, front):
    children, rows, _ = lower.shape
    width = schur.shape[2]
    depth = upper.shape[1]
    cap = 3 * rows // (2 * count)
    slots = count * cap
    steps = len(STEPS)
    full = depth * count
    zs = count // X
    dims = (count, cols, rows, width, depth, cap)
    widths = [width // 4 * number for _, _, number in STEPS]
    half = width // 2
    vmem = pl.BlockSpec(memory_space=pltpu.VMEM)
    hbm = pl.BlockSpec(memory_space=pltpu.HBM)
    dma = pltpu.SemaphoreType.DMA
    scratch = dict(
        lower=pltpu.VMEM(lower.shape, BF16),
        upper=pltpu.VMEM(upper.shape, BF16),
        schur=pltpu.VMEM(schur.shape, F32),
        packed=pltpu.VMEM((children, cols, rows + 16, TILE), BF16),
        wide=pltpu.VMEM((rows, full), BF16),
        panel=[pltpu.VMEM((full, w), BF16) for w in widths],
        square=pltpu.VMEM((rows, rows), BF16),
        hot=pltpu.VMEM((slots, rows), BF16),
        owner=pltpu.VMEM((children, count, rows), BF16),
        rows_info=pltpu.VMEM((8, rows), F32),
        cols_info=pltpu.VMEM((rows, 8), F32),
        place_info=pltpu.VMEM((children, count, TILE), F32),
        scale_col=pltpu.VMEM((rows, TILE), BF16),
        both=pltpu.VMEM((rows, 2 * half), BF16),
        code_out=[pltpu.VMEM((slots, w), jnp.int16) for w in widths],
        code_in=[pltpu.VMEM((slots, w), jnp.int16) for w in widths],
        meta_out=pltpu.VMEM((steps, count, 1, TILE), F32),
        meta_in=pltpu.VMEM((steps, count, 1, TILE), F32),
        meta_flat=pltpu.VMEM((count, TILE), F32),
        spread=pltpu.VMEM((2, TILE, slots), BF16),
        both_in=pltpu.VMEM((slots, 2 * half), BF16),
        local_sem=dma((18,)),
        z_send=dma((steps,)),
        z_recv=dma((steps, zs)),
        x_send=dma((steps,)),
        x_recv=dma((steps, 2, 2)),
        far_recv=dma((steps,)),
        y_send=dma((children, 2, 2, 2)),
        y_recv=dma((children, 2, 2, 2)),
        c_send=dma((children,)),
        c_recv=dma((children,)),
        e_send=dma((steps,)),
        e_recv=dma((steps, max(GROUPS))),
        m_send=dma((steps,)),
        m_recv=dma((steps, max(GROUPS))),
    )
    added = pl.pallas_call(
        functools.partial(kernel, dims),
        out_shape=jax.ShapeDtypeStruct((rows, width), F32),
        in_specs=[hbm, hbm, pl.BlockSpec(memory_space=pltpu.SMEM), vmem, hbm],
        out_specs=vmem,
        scratch_shapes=[scratch],
        compiler_params=pltpu.CompilerParams(
            collective_id=0, has_side_effects=True, vmem_limit_bytes=50 * 2**20
        ),
    )(
        pltpu.with_memory_space_constraint(lower, pltpu.HBM),
        pltpu.with_memory_space_constraint(upper, pltpu.HBM),
        pltpu.with_memory_space_constraint(jnp.swapaxes(tile_mask, 1, 2), pltpu.HBM),
        pltpu.with_memory_space_constraint(row_map, pltpu.HBM),
        schur,
    )
    return front + added


def solution(mesh):
    count, cols = mesh.shape["row"], mesh.shape["col"]
    split = P(None, "row", "col")
    return jax.shard_map(
        functools.partial(shards, count, cols),
        mesh=mesh,
        in_specs=(split, split, split, split, P(None, "row"), P("row", "col")),
        out_specs=P("row", "col"),
        check_vma=False,
    )
```

```python
import functools

import jax
import jax.numpy as jnp
from jax import lax
from jax.experimental import pallas as pl
from jax.experimental.pallas import tpu as pltpu
from jax.sharding import PartitionSpec as P

TILE = 128
X = 4
CORES = 2
STEPS = ((0, 0, 1), (0, 1, 1), (0, 2, 2), (1, 0, 2), (1, 2, 2))
DIRECT = 2
GROUPS = (1, 1, 1, 1, 8)
MESH = pl.DeviceIdType.MESH
F32 = jnp.float32
BF16 = jnp.bfloat16
I32 = jnp.int32


def dot(a, b):
    return jnp.dot(a, b, preferred_element_type=F32)


def iota(shape, dim):
    return lax.broadcasted_iota(I32, shape, dim)


def kernel(
    dims,
    lower_hbm,
    upper_hbm,
    mask_ref,
    map_ref,
    schur_hbm,
    out_ref,
    s,
):
    count, cols, rows, width, depth, cap = dims
    zs = count // X
    ys = cols // CORES
    quarter = width // 4
    slots = count * cap
    steps = len(STEPS)
    me = lax.axis_index("row")
    col = lax.axis_index("col")
    my_z = me // X
    my_x = lax.rem(me, X)
    my_y = col // CORES
    core = lax.rem(col, CORES)
    partner = my_y * CORES + (1 - core)
    lower, upper, schur, packed, wide, panel = s["lower"], s["upper"], s["schur"], s["packed"], s["wide"], s["panel"]
    square, hot, owner = s["square"], s["hot"], s["owner"]
    rows_info, cols_info, place_info = s["rows_info"], s["cols_info"], s["place_info"]
    scale_col, both, both_in = s["scale_col"], s["both"], s["both_in"]
    code_out, code_in, meta_out, meta_in = s["code_out"], s["code_in"], s["meta_out"], s["meta_in"]
    meta_flat, spread = s["meta_flat"], s["spread"]
    local_sem = s["local_sem"]

    barrier = pltpu.get_barrier_semaphore()

    def greet_row(k, carry):
        pl.semaphore_signal(barrier, inc=1, device_id=(lax.rem(me + k, count), col), device_id_type=MESH)
        return carry

    def greet_col(k, carry):
        pl.semaphore_signal(barrier, inc=1, device_id=(me, lax.rem(col + k, cols)), device_id_type=MESH)
        return carry

    lax.fori_loop(1, count, greet_row, 0)
    lax.fori_loop(1, cols, greet_col, 0)

    lower_copy = pltpu.make_async_copy(lower_hbm, lower, local_sem.at[1])
    upper_copy = pltpu.make_async_copy(upper_hbm, upper, local_sem.at[2])
    schur_copy = pltpu.make_async_copy(schur_hbm, schur, local_sem.at[0])
    lower_copy.start()
    upper_copy.start()
    schur_copy.start()

    def remote(source, target, sent, got, device):
        return pltpu.make_async_remote_copy(
            src_ref=source, dst_ref=target, send_sem=sent, recv_sem=got, device_id=device, device_id_type=MESH
        )

    def total(ref, sent, got):
        return remote(ref, ref, sent, got, (me, partner))

    def pack(child):
        for tile in range(rows // TILE):
            at = pl.ds(tile * TILE, TILE)
            second = mask_ref[child, 1, tile]
            packed[child, col, at, :] = jnp.where(
                second == 1, lower[child, at, TILE : 2 * TILE], lower[child, at, 0:TILE]
            )
        row = iota((16, TILE), 0)
        flags = jnp.zeros((16, TILE), F32)
        for tile in range(rows // TILE):
            flags = jnp.where(row == tile, mask_ref[child, 1, tile].astype(F32), flags)
        packed[child, col, pl.ds(rows, 16), :] = flags.astype(BF16)

    def upper_block(step):
        child, first, number = STEPS[step]
        return upper.at[child, :, pl.ds(first * quarter, number * quarter)]

    def panel_block(step, z, x):
        start = pl.multiple_of((z * X + x) * depth, depth)
        return panel[step].at[pl.ds(start, depth), :]

    def nearest(n):
        half = n // 2 + 1
        return half + lax.rem(n, 2) * (zs - 2 * half)

    def z_copy(step, dz):
        z = lax.rem(my_z + dz, zs)
        return remote(
            upper_block(step),
            panel_block(step, my_z, my_x),
            s["z_send"].at[step],
            s["z_recv"].at[step, dz],
            (z * X + my_x, col),
        )

    def behind(i):
        return nearest(i - 1) if i else 0

    def x_copy(step, i, way):
        z = lax.rem(my_z - behind(i) + zs, zs)
        return remote(
            upper_block(step) if i == 0 else panel_block(step, z, my_x),
            panel_block(step, z, my_x),
            s["x_send"].at[step],
            s["x_recv"].at[step, (1 + way) // 2, i % 2],
            (my_z * X + lax.rem(my_x + way + X, X), col),
        )

    def far_copy(step, i, way):
        z = lax.rem(my_z - behind(i) + zs, zs)
        block = panel_block(step, z, lax.rem(my_x - way + X, X))
        return remote(
            block,
            block,
            s["x_send"].at[step],
            s["far_recv"].at[step],
            (my_z * X + lax.rem(my_x + way + X, X), col),
        )

    def send_own(step):
        for way in (1, -1):
            x_copy(step, 0, way).start()
        pltpu.make_async_copy(upper_block(step), panel_block(step, my_z, my_x), local_sem.at[3 + step]).start()

    def send_upper(step):
        def body(n, carry):
            z_copy(step, nearest(n)).start()
            return carry

        lax.fori_loop(0, zs - 1, body, 0)
        send_own(step)

    def pass_upper(step):
        for i in range(1, zs):
            z_copy(step, behind(i)).wait_recv()
            for way in (1, -1):
                x_copy(step, i, way).start()

    def near_x(step, way, part):
        return total(
            panel[step].at[pl.ds(0, zs // 2 * depth), :],
            s["x_send"].at[step],
            s["x_recv"].at[step, (1 + way) // 2, part],
        )

    def x_far(step):
        for way, part in ((1, 0), (-1, 1)):
            near_x(step, way, part).wait_recv()
            for i in range(part, zs, 2):
                far_copy(step, i, way).start()

    def reach(step, way):
        return zs // 2 if (step % 2 == 0) == (way > 0) else zs // 2 - 1

    def hop_copy(step, way, hop):
        z = lax.rem(my_z - way * (hop - 1) + zs, zs)
        block = upper_block(step) if hop == 1 else panel_block(step, z, my_x)
        return remote(
            block,
            panel_block(step, z, my_x),
            s["z_send"].at[step],
            s["z_recv"].at[step, (way * hop) % zs],
            (lax.rem(my_z + way + zs, zs) * X + my_x, col),
        )

    def hop_wait(step, hop):
        for way in (1, -1):
            if hop <= reach(step, way):
                hop_copy(step, way, hop).wait_recv()

    def hop_send(step, hop):
        for way in (1, -1):
            if hop <= reach(step, way):
                hop_copy(step, way, hop).start()

    def hops(hop):
        for step in range(DIRECT, steps):
            hop_wait(step, hop)
            hop_send(step, hop + 1)

    def x_spread(step):
        send_own(step)
        for i in range(1, zs):
            for way in (1, -1):
                x_copy(step, i, way).start()

    def all_x(step):
        return total(
            panel[step].at[pl.ds(0, (X - 1) * zs * depth), :], s["x_send"].at[step], s["far_recv"].at[step]
        )

    def wait_upper(step):
        pltpu.make_async_copy(upper_block(step), panel_block(step, my_z, my_x), local_sem.at[3 + step]).wait()
        near_x(step, 1, 1).wait_recv()
        near_x(step, -1, 0).wait_recv()
        total(
            panel[step].at[pl.ds(0, zs * depth), :], s["x_send"].at[step], s["far_recv"].at[step]
        ).wait_recv()

    middle = rows // 2
    parts = (pl.ds(0, middle), pl.ds(middle, rows + 16 - middle))

    def y_copy(child, way, part, hop):
        block = lax.rem(my_y - way * (hop - 1) + ys, ys) * CORES + core
        ref = packed.at[child, block, parts[part], :]
        return remote(
            ref,
            ref,
            s["y_send"].at[child, (1 + way) // 2, part, hop - 1],
            s["y_recv"].at[child, (1 + way) // 2, part, hop - 1],
            (me, lax.rem(my_y + way + ys, ys) * CORES + core),
        )

    def c_copy(child, behind, part):
        block = lax.rem(my_y - behind + ys, ys) * CORES + core
        ref = packed.at[child, block, parts[part], :]
        return remote(ref, ref, s["c_send"].at[child], s["c_recv"].at[child], (me, partner))

    def send_lower(child):
        for way, part in ((1, 0), (-1, 1), (1, 1), (-1, 0)):
            y_copy(child, way, part, 1).start()
        for part in range(2):
            c_copy(child, 0, part).start()

    def pass_lower(child):
        for way, part in ((1, 0), (-1, 1)):
            y_copy(child, way, part, 1).wait_recv()
            y_copy(child, way, part, 2).start()
            c_copy(child, way, part).start()

    def pass_lower_again(child):
        for way, part in ((1, 1), (-1, 0)):
            y_copy(child, way, part, 1).wait_recv()
            c_copy(child, way, part).start()
        for way, part in ((1, 0), (-1, 1)):
            y_copy(child, way, part, 2).wait_recv()
            c_copy(child, 2 * way, part).start()

    def all_c(child):
        return total(packed.at[child, pl.ds(0, ys)], s["c_send"].at[child], s["c_recv"].at[child])

    def index_rows():
        def strict(b, carry):
            at = pl.ds(pl.multiple_of(b * TILE, TILE), TILE)
            before = iota((TILE, rows), 0) + b * TILE < iota((TILE, rows), 1)
            square[at, :] = jnp.where(before, 1.0, 0.0).astype(BF16)
            return carry

        lax.fori_loop(0, rows // TILE, strict, 0)
        for child in range(2):
            line = map_ref[pl.ds(child, 1), :]
            same = iota((count, rows), 0) == line // rows
            owner[child] = jnp.where(same, 1.0, 0.0).astype(BF16)
        rows_info[...] = jnp.zeros_like(rows_info)
        for child in range(2):
            line = map_ref[pl.ds(child, 1), :]
            hits = owner[child]
            ahead = dot(hits, square[...])
            rank = jnp.sum(ahead * hits.astype(F32), axis=0, keepdims=True)
            spot = lax.rem(line, rows) + 1
            rows_info[pl.ds(4 * child, 1), :] = rank
            rows_info[pl.ds(4 * child + 1, 1), :] = (spot // 32).astype(F32)
            rows_info[pl.ds(4 * child + 2, 1), :] = lax.rem(spot, 32).astype(F32)
            rows_info[pl.ds(4 * child + 3, 1), :] = (line // rows).astype(F32)

    def index_cols():
        def identity(b, carry):
            at = pl.ds(pl.multiple_of(b * TILE, TILE), TILE)
            equal = iota((TILE, rows), 0) + b * TILE == iota((TILE, rows), 1)
            square[at, :] = jnp.where(equal, 1.0, 0.0).astype(BF16)
            return carry

        lax.fori_loop(0, rows // TILE, identity, 0)
        cols_info[...] = lax.dot_general(
            square[...], rows_info[...].astype(BF16), (((1,), (1,)), ((), ())), preferred_element_type=F32
        )
        for child in range(2):
            lane = iota((rows, TILE), 1).astype(F32)
            match = lane - 64.0 == cols_info[:, 4 * child : 4 * child + 1]
            tops = jnp.where(match, cols_info[:, 4 * child + 1 : 4 * child + 2], 0.0).astype(BF16)
            ends = jnp.where(match, cols_info[:, 4 * child + 2 : 4 * child + 3], 0.0).astype(BF16)
            place_info[child] = 32.0 * dot(owner[child], tops) + dot(owner[child], ends)
        slot = iota((TILE, slots), 1).astype(F32)
        inner = slot - cap * jnp.floor((slot + 0.5) * (1.0 / cap))
        lane = iota((TILE, slots), 0).astype(F32)
        spread[0] = jnp.where(lane == inner, 1.0, 0.0).astype(BF16)
        spread[1] = jnp.where(lane - 64.0 == inner, 1.0, 0.0).astype(BF16)

    def build_hot(child):
        flat = rows_info[pl.ds(4 * child + 3, 1), :] * float(cap) + rows_info[pl.ds(4 * child, 1), :]

        def body(b, carry):
            at = pl.ds(pl.multiple_of(b * TILE, TILE), TILE)
            slot = (iota((TILE, rows), 0) + b * TILE).astype(F32)
            hot[at, :] = jnp.where(slot == flat, 1.0, 0.0).astype(BF16)
            return carry

        lax.fori_loop(0, slots // TILE, body, 0)

    def widen(child):
        def body(j, carry):
            flags = packed[child, j, pl.ds(rows, 16), :].astype(F32)
            for tile in range(rows // TILE):
                at = pl.ds(tile * TILE, TILE)
                block = packed[child, j, at, :].astype(F32)
                flag = flags[tile : tile + 1, :]
                left = pl.multiple_of(j * 2 * TILE, TILE)
                right = pl.multiple_of(j * 2 * TILE + TILE, TILE)
                wide[at, pl.ds(left, TILE)] = (block * (1.0 - flag)).astype(BF16)
                wide[at, pl.ds(right, TILE)] = (block * flag).astype(BF16)
            return carry

        lax.fori_loop(0, cols, body, 0)

    def contribute(step):
        child, first, number = STEPS[step]
        cw = number * quarter
        part = rows // 2
        for b in range(2):
            at = pl.ds(b * part, part)
            update = dot(wide[at, :], panel[step][...])
            value = schur[child, at, pl.ds(first * quarter, cw)] - update
            peak = jnp.maximum(jnp.max(jnp.abs(value), axis=1, keepdims=True), 1e-30)
            scale_col[at, :] = jnp.broadcast_to(peak * ((1.0 + 2.0**-8) / 32767.0), (part, TILE)).astype(BF16)
            inverse = 1.0 / scale_col[at, :].astype(F32)
            code = jnp.floor(value * inverse[:, 0:1] + 0.5)
            top = jnp.floor(code * (1.0 / 256.0))
            both[at, 0:cw] = top.astype(BF16)
            both[at, cw : 2 * cw] = (code - 256.0 * top).astype(BF16)
        size = slots // 3
        for b in range(3):
            at = pl.ds(b * size, size)
            moved = dot(hot[at, :], both[:, 0 : 2 * cw])
            code = 256.0 * moved[:, 0:cw] + moved[:, cw : 2 * cw]
            code_out[step][at, :] = code.astype(I32).astype(jnp.int16)
        lane = iota((rows, TILE), 1).astype(F32)
        match = lane == cols_info[:, 4 * child : 4 * child + 1]
        scales = jnp.where(match, scale_col[...].astype(F32), 0.0).astype(BF16)
        meta = dot(owner[child], scales) + place_info[child]
        for t in range(count):
            meta_out[step, t] = meta[t : t + 1, :]

    def rows_of(t):
        return pl.ds(pl.multiple_of(t * cap, 16), cap)

    def shift(n):
        place = n // 2 + lax.rem(n, 2) * (count - 2 - 2 * (n // 2))
        half = place // 2 + 1
        return half + lax.rem(place, 2) * (count - 2 * half)

    def e_copy(step, n, group):
        t = lax.rem(me + shift(n), count)
        return remote(
            code_out[step].at[rows_of(t), :],
            code_in[step].at[rows_of(n), :],
            s["e_send"].at[step],
            s["e_recv"].at[step, group],
            (t, col),
        )

    def m_copy(step, n, group):
        t = lax.rem(me + shift(n), count)
        return remote(
            meta_out.at[step, t], meta_in.at[step, n], s["m_send"].at[step], s["m_recv"].at[step, group], (t, col)
        )

    def own_copies(step):
        return (
            pltpu.make_async_copy(
                code_out[step].at[rows_of(me), :], code_in[step].at[rows_of(count - 1), :], local_sem.at[8 + step]
            ),
            pltpu.make_async_copy(meta_out.at[step, me], meta_in.at[step, count - 1], local_sem.at[13 + step]),
        )

    def exchange(step):
        members = count // GROUPS[step]
        for group in range(GROUPS[step]):

            def body(n, carry):
                m_copy(step, n, group).start()
                e_copy(step, n, group).start()
                return carry

            lax.fori_loop(group * members, min((group + 1) * members, count - 1), body, 0)
        for copy in own_copies(step):
            copy.start()

    def all_codes(step, group, number):
        ref = code_in[step].at[pl.ds(0, number * cap), :]
        return total(ref, s["e_send"].at[step], s["e_recv"].at[step, group])

    def all_meta(step, group, number):
        ref = meta_in.at[step, pl.ds(0, number)]
        return total(ref, s["m_send"].at[step], s["m_recv"].at[step, group])

    def collect(step, group):
        _, first, number = STEPS[step]
        cw = number * quarter
        members = count // GROUPS[step]
        others = members
        if group == GROUPS[step] - 1:
            others = members - 1
            for copy in own_copies(step):
                copy.wait()
        all_meta(step, group, others).wait_recv()
        for m in range(members):
            meta_flat[m : m + 1, :] = meta_in[step, group * members + m]
        flat = meta_flat[0:members, :]
        tops = jnp.floor(flat * (1.0 / 32.0))
        ends = flat - 32.0 * tops
        size = members * cap
        for_place, for_scale = spread[1, :, 0:size], spread[0, :, 0:size]
        places = 32.0 * dot(tops.astype(BF16), for_place) + dot(ends.astype(BF16), for_place)
        scales = dot(flat.astype(BF16), for_scale)
        slot = iota((members, size), 1)
        start = iota((members, size), 0) * cap
        own = (slot >= start) & (slot < start + cap)
        place = jnp.sum(jnp.where(own, places, 0.0), axis=0, keepdims=True)
        scale = jnp.sum(jnp.where(own, scales, 0.0), axis=0, keepdims=True)
        all_codes(step, group, others).wait_recv()
        code = code_in[step][group * size : (group + 1) * size, :].astype(I32)
        both_in[0:size, 0:cw] = (code >> 8).astype(F32).astype(BF16)
        both_in[0:size, cw : 2 * cw] = (code & 255).astype(F32).astype(BF16)
        part = rows // 2
        for b in range(2):
            target = (iota((part, size), 0) + (b * part + 1)).astype(F32)
            pick = jnp.where(target == place, scale, 0.0).astype(BF16)
            at = (pl.ds(b * part, part), pl.ds(first * quarter, cw))
            moved = dot(pick, both_in[0:size, 0 : 2 * cw])
            value = 256.0 * moved[:, 0:cw] + moved[:, cw : 2 * cw]
            if STEPS[step][0] == 0 and group == 0:
                out_ref[at] = value
            else:
                out_ref[at] = out_ref[at] + value

    lower_copy.wait()
    upper_copy.wait()
    pack(0)
    pl.semaphore_wait(barrier, count + cols - 2)
    send_upper(0)
    send_lower(0)
    send_upper(1)
    for step in range(DIRECT, steps):
        hop_send(step, 1)
    pack(1)
    index_rows()
    index_cols()
    pass_upper(0)
    pass_lower(0)
    hops(1)
    pass_upper(1)
    x_far(0)
    pass_lower_again(0)
    send_lower(1)
    hops(2)
    build_hot(0)
    x_far(1)
    hops(3)
    all_c(0).wait_recv()
    widen(0)
    schur_copy.wait()
    wait_upper(0)
    for step in range(DIRECT, steps):
        hop_wait(step, 4)
    x_spread(2)
    contribute(0)
    exchange(0)
    pass_lower(1)
    wait_upper(1)
    contribute(1)
    exchange(1)
    x_far(2)
    x_spread(3)
    pass_lower_again(1)
    wait_upper(2)
    contribute(2)
    exchange(2)
    all_c(1).wait_recv()
    widen(1)
    build_hot(1)
    x_far(3)
    x_spread(4)
    collect(0, 0)
    wait_upper(3)
    contribute(3)
    exchange(3)
    x_far(4)
    collect(1, 0)
    wait_upper(4)
    contribute(4)
    exchange(4)
    for step in range(2, steps):
        for group in range(GROUPS[step]):
            collect(step, group)

    for step in range(steps):
        total(
            panel[step].at[pl.ds(0, (zs - 1) * depth), :], s["z_send"].at[step], s["z_recv"].at[step, 0]
        ).wait_send()
        all_x(step).wait_send()
        all_codes(step, 0, count - 1).wait_send()
        all_meta(step, 0, count - 1).wait_send()
    for child in range(2):
        for part in range(2):
            for way in (1, -1):
                y_copy(child, way, part, 1).wait_send()
            y_copy(child, 1 - 2 * part, part, 2).wait_send()
        all_c(child).wait_send()


def shards(count, cols, schur, lower, upper, tile_mask, row_map, front):
    children, rows, _ = lower.shape
    width = schur.shape[2]
    depth = upper.shape[1]
    cap = 3 * rows // (2 * count)
    slots = count * cap
    steps = len(STEPS)
    full = depth * count
    zs = count // X
    dims = (count, cols, rows, width, depth, cap)
    widths = [width // 4 * number for _, _, number in STEPS]
    half = width // 2
    vmem = pl.BlockSpec(memory_space=pltpu.VMEM)
    hbm = pl.BlockSpec(memory_space=pltpu.HBM)
    dma = pltpu.SemaphoreType.DMA
    scratch = dict(
        lower=pltpu.VMEM(lower.shape, BF16),
        upper=pltpu.VMEM(upper.shape, BF16),
        schur=pltpu.VMEM(schur.shape, F32),
        packed=pltpu.VMEM((children, cols, rows + 16, TILE), BF16),
        wide=pltpu.VMEM((rows, full), BF16),
        panel=[pltpu.VMEM((full, w), BF16) for w in widths],
        square=pltpu.VMEM((rows, rows), BF16),
        hot=pltpu.VMEM((slots, rows), BF16),
        owner=pltpu.VMEM((children, count, rows), BF16),
        rows_info=pltpu.VMEM((8, rows), F32),
        cols_info=pltpu.VMEM((rows, 8), F32),
        place_info=pltpu.VMEM((children, count, TILE), F32),
        scale_col=pltpu.VMEM((rows, TILE), BF16),
        both=pltpu.VMEM((rows, 2 * half), BF16),
        code_out=[pltpu.VMEM((slots, w), jnp.int16) for w in widths],
        code_in=[pltpu.VMEM((slots, w), jnp.int16) for w in widths],
        meta_out=pltpu.VMEM((steps, count, 1, TILE), F32),
        meta_in=pltpu.VMEM((steps, count, 1, TILE), F32),
        meta_flat=pltpu.VMEM((count, TILE), F32),
        spread=pltpu.VMEM((2, TILE, slots), BF16),
        both_in=pltpu.VMEM((slots, 2 * half), BF16),
        local_sem=dma((18,)),
        z_send=dma((steps,)),
        z_recv=dma((steps, zs)),
        x_send=dma((steps,)),
        x_recv=dma((steps, 2, 2)),
        far_recv=dma((steps,)),
        y_send=dma((children, 2, 2, 2)),
        y_recv=dma((children, 2, 2, 2)),
        c_send=dma((children,)),
        c_recv=dma((children,)),
        e_send=dma((steps,)),
        e_recv=dma((steps, max(GROUPS))),
        m_send=dma((steps,)),
        m_recv=dma((steps, max(GROUPS))),
    )
    added = pl.pallas_call(
        functools.partial(kernel, dims),
        out_shape=jax.ShapeDtypeStruct((rows, width), F32),
        in_specs=[hbm, hbm, pl.BlockSpec(memory_space=pltpu.SMEM), vmem, hbm],
        out_specs=vmem,
        scratch_shapes=[scratch],
        compiler_params=pltpu.CompilerParams(
            collective_id=0, has_side_effects=True, vmem_limit_bytes=50 * 2**20
        ),
    )(
        pltpu.with_memory_space_constraint(lower, pltpu.HBM),
        pltpu.with_memory_space_constraint(upper, pltpu.HBM),
        pltpu.with_memory_space_constraint(jnp.swapaxes(tile_mask, 1, 2), pltpu.HBM),
        pltpu.with_memory_space_constraint(row_map, pltpu.HBM),
        schur,
    )
    return front + added


def solution(mesh):
    count, cols = mesh.shape["row"], mesh.shape["col"]
    split = P(None, "row", "col")
    return jax.shard_map(
        functools.partial(shards, count, cols),
        mesh=mesh,
        in_specs=(split, split, split, split, P(None, "row"), P("row", "col")),
        out_specs=P("row", "col"),
        check_vma=False,
    )
```
